256 devices in a mesh: freq: 8 (over x, core), mode: 32 (over y, z).
Axes of the slice: x: 4, y: 4, z: 8, core: 2. Of those that a mesh axis runs over, the one named last changes fastest.
Arguments:
- mode_shapes: bfloat16 [6144, 12288], P(None, 'mode'), may hold values from -0.109375 to 0.109375
- modal_freq: float32 [12288], P('mode'), may hold values from 0.5 to 4
- damping: float32 [12288], P('mode'), may hold values from 0.05 to 0.2
- excitation: float32 [32], P('freq'), parts along dimension 0, may hold values from 0.5 to 4
- modal_load: float32 [12288, 32, 2, 64], P('mode', 'freq'), parts along dimension 1, may hold values from -6 to 6
- attach: int32 [32, 96], replicated, may hold values from 0 to 6143
- row_count: int32 [32], P('mode'), may hold values from 48 to 384, as said below
- otm: bfloat16 [32, 384, 96], P('mode'), may hold values from -0.625 to 0.625
Outputs:
- csd: bfloat16 [32, 32, 2, 384, 384], P('mode', 'freq'), parts along dimension 1
- joint_csd: bfloat16 [32, 32, 2, 128, 384], P('mode', 'freq'), parts along dimension 1
The draws below stay inside these ranges and needn't reach their ends.
There are 8 independent parts, one for each index of `freq`. The reference program is written for one: setup_inputs(seed, part) draws one part's arguments, and reference() takes and returns one part's arrays. A program takes and returns all parts, laid end to end along the dimension named above; an argument that names none is the same for every part. Nothing has to cross between parts.
Inputs may be any that keep to these rules, and one draw needn't show every extreme that they name: `row_count`: at least one component has exactly 384 rows in every draw.
All inputs are finite; a program needn't handle non-finite values.
Results may differ from the reference program's by a relative error of at most 0.008.
Values may be sent and summed in bfloat16 or wider, within the bound.
A program may use at most 128 MiB of HBM per device.

```python
import math
import jax
import jax.numpy as jnp

MODES = 12288
IFACE = 6144
K = 64
FREQ_PART = 4
COMPS = 32
ATT = 96
ROWS_MAX = 384
CROSS = 128


def draw_row_count(key, part):
    base_key = jax.random.fold_in(key, 11)
    first_key, second_key = jax.random.split(base_key)
    spread = jax.random.randint(first_key, (COMPS,), 0, 64)
    lowest = ROWS_MAX // 8
    counts = lowest + spread * spread * (ROWS_MAX - lowest) // 3969
    chosen = jax.random.randint(second_key, (), 0, COMPS)
    counts = jnp.where(jnp.arange(COMPS) == chosen, ROWS_MAX, counts)
    return counts.astype(jnp.int32)


def plant(drawn, stream_key, least, top_value):
    dims = drawn.shape
    spot = [jax.random.randint(jax.random.fold_in(stream_key, axis), (), 0, dims[axis]) for axis in range(len(dims))]
    drawn = drawn.at[tuple(spot)].set(least)
    longest = dims.index(max(dims))
    spot[longest] = (spot[longest] + 1) % dims[longest]
    return drawn.at[tuple(spot)].set(top_value)


def strengthened(entries, rng, source, target, blocks, factor):
    owner, partner = [(jnp.arange(entries.shape[position]) // (entries.shape[position] // blocks)).reshape([-1 if axis == position else 1 for axis in range(entries.ndim)]) for position in (source, target)]
    chosen = jax.random.permutation(rng, blocks)[partner]
    strong = (owner == chosen) | (owner == (partner + blocks // 2) % blocks)
    return jnp.where(strong, factor * entries, entries)


def shard_levels(own_key, shape, cuts, least, top_value):
    def one(position, shards_of):
        draws = jax.random.uniform(jax.random.fold_in(jax.random.fold_in(own_key, 6), position), (shards_of,), jnp.float32, least / len(cuts), top_value / len(cuts))
        return jnp.repeat(jnp.exp(draws), shape[position] // shards_of).reshape((-1,) + (1,) * (len(shape) - position - 1))

    level = one(*cuts[0])
    for cut in cuts[1:]:
        level = level * one(*cut)
    return level


def normal_values(rng, extent, width, limit, cuts=(), held_as=jnp.bfloat16):
    values = width * jax.random.normal(rng, extent, jnp.float32)
    if cuts:
        values = values * shard_levels(rng, extent, cuts, -0.22, 0.18)
    return jnp.clip(values, -limit, limit).astype(held_as)


def noise_with(rng, shape, scale, limit, cuts, heavy, held_as=jnp.bfloat16):
    result = scale * jax.random.normal(rng, shape, jnp.float32)
    if cuts:
        result = result * shard_levels(rng, shape, cuts, -0.22, 0.18)
    return jnp.clip(strengthened(result, jax.random.fold_in(rng, 3), *heavy), -limit, limit).astype(held_as)


def setup_inputs(seed: int = 0, part: int = 0) -> dict:
    key_of = jax.random.split(jax.random.key(seed), 9)
    part_keys = jax.random.split(jax.random.fold_in(key_of[8], part), 9)
    mode_shapes = noise_with(key_of[0], (IFACE, MODES), MODES ** -0.5, 0.109375, ((1, 32),), (1, 0, 32, 2.75))
    modal_freq = jnp.clip(jnp.exp(math.log(4.0) - 2.0794415 * jax.random.uniform(key_of[1], (MODES,), jnp.float32) ** shard_levels(key_of[1], (MODES,), ((0, 32),), -0.2, 0.2)), 0.5, 4.0)
    damping = jnp.clip(jnp.exp(math.log(0.2) - 1.3862944 * jax.random.uniform(key_of[2], (MODES,), jnp.float32) ** shard_levels(key_of[2], (MODES,), ((0, 32),), -0.2, 0.2)), 0.05, 0.2)
    excitation = jnp.clip(jax.random.uniform(part_keys[3], (FREQ_PART,), jnp.float32, 0.5, 4.0), 0.5, 4.0)
    modal_load = normal_values(part_keys[4], (MODES, FREQ_PART, 2, K), 1.0, 6.0, ((0, 32),), jnp.float32)
    attach = plant(jax.random.randint(key_of[5], (COMPS, ATT), 0, IFACE), jax.random.fold_in(key_of[5], 1), 0, IFACE - 1).astype(jnp.int32)
    row_count = draw_row_count(jax.random.fold_in(key_of[8], 71), part)
    otm = normal_values(key_of[7], (COMPS, ROWS_MAX, ATT), ATT ** -0.5, 0.625, ((0, 32),))
    return dict(mode_shapes=mode_shapes, modal_freq=modal_freq, damping=damping, excitation=excitation, modal_load=modal_load, attach=attach, row_count=row_count, otm=otm)


def reference(mode_shapes, modal_freq, damping, excitation, modal_load, attach, row_count, otm):
    omega_sq = modal_freq * modal_freq
    real_part = omega_sq[:, None] - (excitation * excitation)[None, :]
    imag_part = 2.0 * damping[:, None] * modal_freq[:, None] * excitation[None, :]
    denom = real_part * real_part + imag_part * imag_part
    frf_re = (omega_sq[:, None] * real_part / denom)[:, :, None]
    frf_im = (-omega_sq[:, None] * imag_part / denom)[:, :, None]
    load_re = modal_load[:, :, 0, :]
    load_im = modal_load[:, :, 1, :]
    resp_re = frf_re * load_re - frf_im * load_im
    resp_im = frf_re * load_im + frf_im * load_re
    modal_resp = jnp.stack([resp_re, resp_im], axis=2).astype(jnp.bfloat16)
    modal_resp = modal_resp.reshape(MODES, FREQ_PART * 2 * K)
    iface_resp = jnp.dot(mode_shapes, modal_resp, preferred_element_type=jnp.float32).astype(jnp.bfloat16)
    picked = jnp.take(iface_resp, attach.reshape(-1).astype(jnp.int32), axis=0).reshape(COMPS, ATT, FREQ_PART * 2 * K)
    row_mask = jnp.arange(ROWS_MAX, dtype=jnp.int32)[None, :] < row_count[:, None]
    factor = jnp.einsum("cra,caj->crj", otm.astype(jnp.float32), picked.astype(jnp.float32))
    factor = jnp.where(row_mask[:, :, None], factor, 0.0).astype(jnp.bfloat16)
    zmat = factor.reshape(COMPS, ROWS_MAX, FREQ_PART, 2 * K).astype(jnp.float32)
    wmat = jnp.concatenate([zmat[..., K:], -zmat[..., :K]], axis=-1)
    auto_re = jnp.einsum("crfk,csfk->cfrs", zmat, zmat) / K
    auto_im = jnp.einsum("crfk,csfk->cfrs", wmat, zmat) / K
    csd = jnp.stack([auto_re, auto_im], axis=2).astype(jnp.bfloat16)
    partner = jnp.concatenate([zmat[1:], jnp.zeros_like(zmat[:1])], axis=0)
    joint_re = jnp.einsum("crfk,csfk->cfrs", zmat[:, :CROSS], partner) / K
    joint_im = jnp.einsum("crfk,csfk->cfrs", wmat[:, :CROSS], partner) / K
    joint_csd = jnp.stack([joint_re, joint_im], axis=2).astype(jnp.bfloat16)
    return (csd, joint_csd)
```

```python
import functools

import jax
import jax.numpy as jnp
from jax import lax
from jax.experimental import pallas as pl
from jax.experimental.pallas import tpu as pltpu
from jax.sharding import PartitionSpec as P

MESH = pl.DeviceIdType.MESH
F32, BF16 = jnp.float32, jnp.bfloat16
NY, NZ = 4, 8
COMPS, ATT, LINES = 32, 96, 4
CROSS = 128
CHUNKS = (("z", 0, 24), ("z", 24, 24), ("y", 48, 24), ("y", 72, 24))
SIZE = {"y": NY, "z": NZ}


def partial_kernel(freq_ref, damp_ref, exc_ref, load_ref, attach_ref, shapes_ref, out_ref, held, resp, whole, sems):
    pieces = sems.shape[0]
    rows = held.shape[0] // pieces
    copies = []
    for piece in range(pieces):
        part = pl.ds(piece * rows, rows)
        copies.append(pltpu.make_async_copy(shapes_ref.at[part], held.at[part], sems.at[piece]))
        copies[-1].start()
    omega = freq_ref[...]
    omega_sq = omega * omega
    for line in range(LINES):
        exc = exc_ref[line]
        a = omega_sq - exc * exc
        b = 2.0 * damp_ref[...] * omega * exc
        denom = a * a + b * b
        frf_re = omega_sq * a / denom
        frf_im = -omega_sq * b / denom
        load_re = load_ref[pl.ds(line * 128, 64), :]
        load_im = load_ref[pl.ds(line * 128 + 64, 64), :]
        resp[pl.ds(line * 128, 64), :] = (frf_re * load_re - frf_im * load_im).astype(BF16)
        resp[pl.ds(line * 128 + 64, 64), :] = (frf_re * load_im + frf_im * load_re).astype(BF16)
    for piece in range(pieces):
        copies[piece].wait()
    steps = 16
    tall = held.shape[0] // steps

    def product(step, carry):
        base = pl.multiple_of(step * tall, tall)
        block = lax.dot_general(
            held[pl.ds(base, tall), :], resp[...], (((1,), (1,)), ((), ())), preferred_element_type=F32
        )
        for line in range(LINES):
            whole[pl.ds(base * LINES + line, tall, stride=LINES), :] = block[:, line * 128 : line * 128 + 128]
        return carry

    lax.fori_loop(0, steps, product, 0)
    unroll = 16

    def gather(step, carry):
        for k in range(unroll):
            row = step * unroll + k
            source = attach_ref[row] * LINES
            out_ref[pl.ds(pl.multiple_of(row * LINES, LINES), LINES), :] = whole[
                pl.ds(pl.multiple_of(source, LINES), LINES), :
            ]
        return carry

    lax.fori_loop(0, COMPS * ATT // unroll, gather, 0)


def plan():
    place, total = {}, 0
    for index, (first, start, rows) in enumerate(CHUNKS):
        order = (first, "y" if first == "z" else "z")
        for phase in range(2):
            n = SIZE[order[phase]]
            inner = SIZE[order[1]] if phase == 0 else 1
            for step in range(n // 2, 0, -1):
                size = inner * rows * LINES
                if step == n // 2:
                    size //= 2
                for side in range(2):
                    place[(index, phase, side, step)] = (len(place), total, size)
                    total += size
    return place, total


PLACE, TOTAL = plan()
ORDER = None


def default_order():
    events = []
    for index, (first, start, rows) in enumerate(CHUNKS):
        order = (first, "y" if first == "z" else "z")
        clock = 0.0
        for phase in range(2):
            n = SIZE[order[phase]]
            big = (14.0 / 4 if order[0] == "z" else 12.0 / 2) if phase == 0 else 2.0
            for step in range(n // 2, -1, -1):
                events.append((clock + 0.01 * index, index, phase, step))
                clock += big * (0.5 if step == n // 2 else 1.0) if step else 0.0
    return [e[1:] for e in sorted(events)]


def reduce_kernel(part_ref, otm_ref, count_ref, own_ref, next_ref, otm_out, otm_next_out,
                  sent, got, held, total, final, otm_mine, otm_got, pick, pick_got, wide,
                  send_sems, recv_sems):
    me = lax.axis_index("mode")
    y, z = me // NZ, lax.rem(me, NZ)
    at = {"y": y, "z": z}

    def device(axis, offset):
        if axis == "z":
            return y * NZ + lax.rem(z + offset + NZ, NZ)
        return lax.rem(y + offset + NY, NY) * NZ + z

    before = lax.rem(me + NY * NZ - 1, NY * NZ)
    after = lax.rem(me + 1, NY * NZ)
    barrier = pltpu.get_barrier_semaphore()
    for peer in (device("z", 1), device("z", -1), device("y", 1), device("y", -1), before, after):
        pl.semaphore_signal(barrier, inc=1, device_id={"mode": peer}, device_id_type=MESH)
    pl.semaphore_wait(barrier, 6)

    count = count_ref[0]
    keep = lax.broadcasted_iota(jnp.int32, otm_ref.shape, 1) < count
    masked = jnp.where(keep, otm_ref[...].astype(F32), 0.0).astype(BF16)
    otm_mine[...] = masked
    otm_out[...] = masked
    base = len(PLACE)
    otm_copy = pltpu.make_async_remote_copy(
        src_ref=otm_mine, dst_ref=otm_got, send_sem=send_sems.at[base], recv_sem=recv_sems.at[base],
        device_id={"mode": before}, device_id_type=MESH)
    otm_copy.start()

    copies, tails = {}, []

    def event(index, phase, step):
        first, start, rows = CHUNKS[index]
        order = (first, "y" if first == "z" else "z")
        axis, other = order[phase], order[1 - phase]
        n = SIZE[axis]
        inner = SIZE[order[1]] if phase == 0 else 1
        tall = rows * LINES

        def own(dest, item):
            if phase == 0:
                unit = item * NZ + dest if axis == "z" else dest * NZ + item
                return part_ref[pl.ds(pl.multiple_of(unit * (ATT * LINES) + start * LINES, 8), tall), :]
            return held[pl.ds(pl.multiple_of((index * NZ + dest) * 96, 8), tall), :]

        def rows_at(ref, offset, item):
            return ref.at[pl.ds(pl.multiple_of(offset + item * tall, 16), tall), :]

        if step == 0:
            places = [PLACE[(index, phase, side, 1)] for side in range(2)]
            for side in range(2):
                copies[(index, phase, side, 1)].wait_recv()

            def add(item, carry):
                value = own(at[axis], item)
                for side in range(2):
                    value = value + rows_at(got, places[side][1], item)[...].astype(F32)
                if phase == 0:
                    held[pl.ds(pl.multiple_of((index * NZ + item) * 96, 8), tall), :] = value
                else:
                    pick[pl.ds(start * LINES, tall), :] = value.astype(BF16)
                return carry

            if phase == 0:
                lax.fori_loop(0, inner, add, 0)
            else:
                add(0, 0)
                slot = base + 1 + index
                part = pl.ds(start * LINES, tall)
                copy = pltpu.make_async_remote_copy(
                    src_ref=pick.at[part], dst_ref=pick_got.at[part], send_sem=send_sems.at[slot],
                    recv_sem=recv_sems.at[slot], device_id={"mode": before}, device_id_type=MESH)
                copy.start()
                tails.append(copy)
            return

        for side in range(2):
            sign = 1 if side == 0 else -1
            number, offset, size = PLACE[(index, phase, side, step)]
            dest = lax.rem(at[axis] + sign * step + n, n)
            if step == n // 2:
                if inner == 1:
                    half = tall // 2
                    value = held[pl.ds(pl.multiple_of((index * NZ + dest) * 96 + side * half, 8), half), :]
                    sent[pl.ds(offset, half), :] = value.astype(BF16)
                else:
                    def fill(item, carry):
                        rows_at(sent, offset, item)[...] = own(dest, item + side * (inner // 2)).astype(BF16)
                        return carry

                    lax.fori_loop(0, inner // 2, fill, 0)
            else:
                copies[(index, phase, side, step + 1)].wait_recv()
                arrived = PLACE[(index, phase, side, step + 1)][1]
                if step + 1 == n // 2:
                    if inner == 1:
                        half = tall // 2
                        lo, hi = (0, half) if side == 0 else (half, 0)
                        with_, without = (0, half) if side == 0 else (half, 0)
                        src = (index * NZ + dest) * 96
                        value = held[pl.ds(pl.multiple_of(src + with_, 8), half), :]
                        value = value + got[pl.ds(arrived, half), :].astype(F32)
                        sent[pl.ds(offset + with_, half), :] = value.astype(BF16)
                        value = held[pl.ds(pl.multiple_of(src + without, 8), half), :]
                        sent[pl.ds(offset + without, half), :] = value.astype(BF16)
                    else:
                        half = inner // 2

                        def fill(item, carry):
                            value = own(dest, item + side * half) + rows_at(got, arrived, item)[...].astype(F32)
                            rows_at(sent, offset, item + side * half)[...] = value.astype(BF16)
                            rows_at(sent, offset, item + (1 - side) * half)[...] = own(
                                dest, item + (1 - side) * half
                            ).astype(BF16)
                            return carry

                        lax.fori_loop(0, half, fill, 0)
                else:
                    def fill(item, carry):
                        value = own(dest, item) + rows_at(got, arrived, item)[...].astype(F32)
                        rows_at(sent, offset, item)[...] = value.astype(BF16)
                        return carry

                    if inner == 1:
                        fill(0, 0)
                    else:
                        lax.fori_loop(0, inner, fill, 0)
            part = pl.ds(offset, size)
            copy = pltpu.make_async_remote_copy(
                src_ref=sent.at[part], dst_ref=got.at[part], send_sem=send_sems.at[number],
                recv_sem=recv_sems.at[number], device_id={"mode": device(axis, sign)}, device_id_type=MESH)
            copy.start()
            copies[(index, phase, side, step)] = copy

    for index, phase, step in default_order():
        event(index, phase, step)
    for line in range(LINES):
        pass
    wide[...] = pick[...].astype(F32)
    for line in range(LINES):
        own_ref[line] = wide[pl.ds(line, ATT, stride=LINES), :].astype(BF16)
    otm_copy.wait_recv()
    otm_next_out[...] = otm_got[...]
    for copy in tails:
        copy.wait_recv()
    wide[...] = jnp.where(me == NY * NZ - 1, 0.0, pick_got[...].astype(F32))
    for line in range(LINES):
        next_ref[line] = wide[pl.ds(line, ATT, stride=LINES), :].astype(BF16)
    for copy in [*copies.values(), *tails, otm_copy]:
        copy.wait_send()


def spectra_kernel(own_ref, next_ref, otm_ref, otm_next_ref, csd_ref, joint_ref):
    def factor(otm, picked):
        return lax.dot_general(otm, picked, (((0,), (0,)), ((), ())), preferred_element_type=F32).astype(BF16)

    def spectra(left, right):
        return lax.dot_general(left, right, (((1,), (1,)), ((), ())), preferred_element_type=F32) * (1.0 / 64.0)

    z_here = factor(otm_ref[...], own_ref[0])
    z_next = factor(otm_next_ref[...], next_ref[0])
    lane = lax.broadcasted_iota(jnp.int32, z_here.shape, 1)
    turned = pltpu.roll(z_here.astype(F32), 64, 1)
    w_here = jnp.where(lane < 64, turned, -turned).astype(BF16)
    csd_ref[0, 0, 0] = spectra(z_here, z_here).astype(BF16)
    csd_ref[0, 0, 1] = spectra(w_here, z_here).astype(BF16)
    joint_ref[0, 0, 0] = spectra(z_here[:CROSS], z_next).astype(BF16)
    joint_ref[0, 0, 1] = spectra(w_here[:CROSS], z_next).astype(BF16)


def per_device(mode_shapes, modal_freq, damping, excitation, modal_load, attach, row_count, otm):
    iface, modes = mode_shapes.shape
    rows_max, width = otm.shape[1], modal_load.shape[3]
    columns = LINES * 2 * width
    load = modal_load.transpose(1, 2, 3, 0).reshape(columns, modes)
    otm_t = otm[0].T
    vmem = pl.BlockSpec(memory_space=pltpu.VMEM)
    smem = pl.BlockSpec(memory_space=pltpu.SMEM)
    partial = pl.pallas_call(
        partial_kernel,
        out_shape=jax.ShapeDtypeStruct((COMPS * ATT * LINES, 128), F32),
        in_specs=[vmem, vmem, smem, vmem, smem, pl.BlockSpec(memory_space=pl.ANY)],
        out_specs=vmem,
        scratch_shapes=[
            pltpu.VMEM((iface, modes), BF16),
            pltpu.VMEM((columns, modes), BF16),
            pltpu.VMEM((iface * LINES, 128), F32),
            pltpu.SemaphoreType.DMA((8,)),
        ],
        compiler_params=pltpu.CompilerParams(vmem_limit_bytes=48 << 20),
        name="partial",
    )(modal_freq[None, :], damping[None, :], excitation, load, attach.reshape(-1), mode_shapes)
    slots = len(PLACE) + 1 + len(CHUNKS)
    own, following, otm_here, otm_next = pl.pallas_call(
        reduce_kernel,
        out_shape=[
            jax.ShapeDtypeStruct((LINES, ATT, 128), BF16),
            jax.ShapeDtypeStruct((LINES, ATT, 128), BF16),
            jax.ShapeDtypeStruct((ATT, rows_max), BF16),
            jax.ShapeDtypeStruct((ATT, rows_max), BF16),
        ],
        in_specs=[vmem, vmem, smem],
        out_specs=[vmem] * 4,
        scratch_shapes=[
            pltpu.VMEM((TOTAL, 128), BF16),
            pltpu.VMEM((TOTAL, 128), BF16),
            pltpu.VMEM((len(CHUNKS) * NZ * 96, 128), F32),
            pltpu.VMEM((8, 128), F32),
            pltpu.VMEM((8, 128), F32),
            pltpu.VMEM((ATT, rows_max), BF16),
            pltpu.VMEM((ATT, rows_max), BF16),
            pltpu.VMEM((ATT * LINES, 128), BF16),
            pltpu.VMEM((ATT * LINES, 128), BF16),
            pltpu.VMEM((ATT * LINES, 128), F32),
            pltpu.SemaphoreType.DMA((slots,)),
            pltpu.SemaphoreType.DMA((slots,)),
        ],
        compiler_params=pltpu.CompilerParams(
            vmem_limit_bytes=40 << 20, collective_id=0, has_side_effects=True
        ),
        name="reduce",
    )(partial, otm_t, row_count)
    by_line = pl.BlockSpec((1, ATT, 128), lambda f: (f, 0, 0))
    whole = pl.BlockSpec((ATT, rows_max), lambda f: (0, 0))
    return tuple(
        pl.pallas_call(
            spectra_kernel,
            grid=(LINES,),
            out_shape=[
                jax.ShapeDtypeStruct((1, LINES, 2, rows_max, rows_max), BF16),
                jax.ShapeDtypeStruct((1, LINES, 2, CROSS, rows_max), BF16),
            ],
            in_specs=[by_line, by_line, whole, whole],
            out_specs=[
                pl.BlockSpec((1, 1, 2, rows_max, rows_max), lambda f: (0, f, 0, 0, 0)),
                pl.BlockSpec((1, 1, 2, CROSS, rows_max), lambda f: (0, f, 0, 0, 0)),
            ],
            name="spectra",
        )(own, following, otm_here, otm_next)
    )


def solution(mesh):
    return jax.shard_map(
        per_device,
        mesh=mesh,
        in_specs=(
            P(None, "mode"),
            P("mode"),
            P("mode"),
            P("freq"),
            P("mode", "freq", None, None),
            P(),
            P("mode"),
            P("mode", None, None),
        ),
        out_specs=(P("mode", "freq", None, None, None), P("mode", "freq", None, None, None)),
        check_vma=False,
    )
```

```python
import jax
import jax.numpy as jnp
from jax import lax
from jax.experimental import pallas as pl
from jax.experimental.pallas import tpu as pltpu
from jax.sharding import PartitionSpec as P

MESH = pl.DeviceIdType.MESH
F32, BF16 = jnp.float32, jnp.bfloat16
NY, NZ = 4, 8
SIZE = {"y": NY, "z": NZ}
OTHER = {"y": "z", "z": "y"}
COMPS, ATT, LINES, CROSS = 32, 96, 4, 128
PIECES = 4
CHUNKS = (
    ("z", 0, 16), ("z", 16, 16), ("y", 32, 12), ("y", 44, 28), ("y", 72, 24),
)
ORDER = (
    (0, 4), (1, 4), (2, 2), (3, 2), (4, 2), (0, 3), (1, 3), (2, 1), (3, 1), (0, 2), (4, 1), (1, 2), (2, 0),
    (0, 1), (1, 1), (3, 0), (2, -1), (0, 0), (1, 0), (4, 0), (0, -1), (1, -1), (3, -1), (4, -1),
)
TALL = max(rows for _, _, rows in CHUNKS) * LINES


def plan():
    place, total = {}, 0
    for index, (first, _, rows) in enumerate(CHUNKS):
        n, m, tall = SIZE[first], SIZE[OTHER[first]], rows * LINES
        for hop in range(n // 2, 0, -1):
            size = m * tall // (2 if hop == n // 2 else 1)
            for side in range(2):
                place[(index, hop, side)] = (len(place), total, size)
                total += size
        for step in range(1, m):
            place[(index, "direct", step)] = (len(place), total, tall)
            total += tall
    return place, total


PLACE, TOTAL = plan()
SLOTS = len(PLACE) + 1 + len(CHUNKS)


def kernel(freq_hbm, damp_hbm, exc_hbm, load_hbm, attach, count_smem, otm_hbm, shapes_hbm, csd_ref, joint_ref,
           freq, damp, exc_smem, load, otm, shapes, resp, whole, own, mine, sent, got,
           otm_got, pick, pick_got, wide, in_sems, send_sems, recv_sems):
    me = lax.axis_index("mode")
    at = {"y": me // NZ, "z": lax.rem(me, NZ)}

    def device(axis, offset):
        if axis == "z":
            return at["y"] * NZ + lax.rem(at["z"] + offset + NZ, NZ)
        return lax.rem(at["y"] + offset + NY, NY) * NZ + at["z"]

    before = lax.rem(me + NY * NZ - 1, NY * NZ)
    after = lax.rem(me + 1, NY * NZ)
    barrier = pltpu.get_barrier_semaphore()
    peers = [device("z", step) for step in range(1, NZ)] + [device("y", step) for step in range(1, NY)]
    for peer in (*peers, before, after):
        pl.semaphore_signal(barrier, inc=1, device_id={"mode": peer}, device_id_type=MESH)

    small = [(freq_hbm, freq), (damp_hbm, damp), (exc_hbm, exc_smem), (load_hbm, load), (otm_hbm, otm)]
    rows = shapes.shape[0] // PIECES
    parts = [pl.ds(piece * rows, rows) for piece in range(PIECES)]
    loads = [pltpu.make_async_copy(src, dst, in_sems.at[k]) for k, (src, dst) in enumerate(small)]
    loads += [
        pltpu.make_async_copy(shapes_hbm.at[part], shapes.at[part], in_sems.at[len(small) + k])
        for k, part in enumerate(parts)
    ]
    for copy in loads:
        copy.start()
    for copy in loads[:4]:
        copy.wait()
    omega = freq[...].reshape(1, -1)
    ratio = damp[...].reshape(1, -1)
    omega_sq = omega * omega
    for line in range(LINES):
        exc = exc_smem[line]
        a = omega_sq - exc * exc
        b = 2.0 * ratio * omega * exc
        denom = a * a + b * b
        frf_re = omega_sq * a / denom
        frf_im = -omega_sq * b / denom
        load_re = load[pl.ds(line * 128, 64), :]
        load_im = load[pl.ds(line * 128 + 64, 64), :]
        resp[pl.ds(line * 128, 64), :] = (frf_re * load_re - frf_im * load_im).astype(BF16)
        resp[pl.ds(line * 128 + 64, 64), :] = (frf_re * load_im + frf_im * load_re).astype(BF16)
    for piece in range(PIECES):
        loads[len(small) + piece].wait()
        block = lax.dot_general(
            shapes[parts[piece], :], resp[...], (((1,), (1,)), ((), ())), preferred_element_type=F32
        )
        for line in range(LINES):
            whole[pl.ds(piece * rows * LINES + line, rows, stride=LINES), :] = block[:, line * 128 : line * 128 + 128]
    loads[4].wait()
    keep = lax.broadcasted_iota(jnp.int32, otm.shape, 1) < count_smem[0]
    otm[...] = jnp.where(keep, otm[...].astype(F32), 0.0).astype(BF16)

    pl.semaphore_wait(barrier, len(peers) + 2)
    copies, tails = {}, []
    table = whole.reshape(whole.shape[0] // LINES, LINES, 128)

    def send(key, place, target, source=sent, dest=got):
        number, offset, size = place
        part = pl.ds(offset, size)
        copy = pltpu.make_async_remote_copy(
            src_ref=source.at[part], dst_ref=dest.at[part], send_sem=send_sems.at[number],
            recv_sem=recv_sems.at[number], device_id={"mode": target}, device_id_type=MESH)
        copy.start()
        copies[key] = copy
        return copy

    def event(index, hop):
        first, start, rows = CHUNKS[index]
        other = OTHER[first]
        n, m, tall = SIZE[first], SIZE[other], rows * LINES

        def block(offset, item):
            return pl.ds(pl.multiple_of(offset + item * tall, 16), tall)

        def gather(dest, item, slot):
            unit = item * NZ + dest if first == "z" else dest * NZ + item
            base = pl.multiple_of(slot * tall, 16)
            for row in range(rows):
                source = attach[unit, start + row]
                own[pl.ds(base + row * LINES, LINES), :] = table[source]

        if hop > 0:
            half = m // 2
            dests = [lax.rem(at[first] + (hop if side == 0 else n - hop), n) for side in range(2)]

            def fetch(low, high):
                def body(item, carry):
                    for side in range(2):
                        gather(dests[side], item + side * low, side * m + item + side * low)
                    return carry

                lax.fori_loop(0, high, body, 0)

            if hop == n // 2:
                fetch(half, half)
            else:
                fetch(0, m)
            for side in range(2):
                place = PLACE[(index, hop, side)]
                if hop == n // 2:
                    def fill(item, carry):
                        sent[block(place[1], item), :] = own[block(0, side * (m + half) + item), :].astype(BF16)
                        return carry

                    lax.fori_loop(0, half, fill, 0)
                else:
                    copies[(index, hop + 1, side)].wait_recv()
                    arrived = PLACE[(index, hop + 1, side)][1]
                    short = hop + 1 == n // 2
                    skip = side * half if short else 0

                    def fill(item, carry):
                        value = own[block(0, side * m + skip + item), :] + got[block(arrived, item), :].astype(F32)
                        sent[block(place[1], skip + item), :] = value.astype(BF16)
                        if short:
                            rest = (1 - side) * half + item
                            sent[block(place[1], rest), :] = own[block(0, side * m + rest), :].astype(BF16)
                        return carry

                    lax.fori_loop(0, half if short else m, fill, 0)
                send((index, hop, side), place, device(first, 1 if side == 0 else -1))
        elif hop == 0:
            def body(item, carry):
                gather(at[first], item, item)
                return carry

            lax.fori_loop(0, m, body, 0)
            arrived = [PLACE[(index, 1, side)][1] for side in range(2)]
            for side in range(2):
                copies[(index, 1, side)].wait_recv()

            def value(item):
                here = own[block(0, item), :]
                for side in range(2):
                    here = here + got[block(arrived[side], item), :].astype(F32)
                return here

            for step in sorted(range(1, m), key=lambda step: -min(step, m - step)):
                place = PLACE[(index, "direct", step)]
                sent[pl.ds(place[1], tall), :] = value(lax.rem(at[other] + step, m)).astype(BF16)
                send((index, "direct", step), place, device(other, step))
            mine[pl.ds(start * LINES, tall), :] = value(at[other])
        else:
            here = mine[pl.ds(start * LINES, tall), :]
            for step in range(1, m):
                copies[(index, "direct", step)].wait_recv()
                here = here + got[pl.ds(PLACE[(index, "direct", step)][1], tall), :].astype(F32)
            pick[pl.ds(start * LINES, tall), :] = here.astype(BF16)
            place = (len(PLACE) + 1 + index, start * LINES, tall)
            tails.append(send((index, "pick"), place, before, pick, pick_got))

    for number, (index, hop) in enumerate(ORDER):
        event(index, hop)
        if number == 4:
            otm_copy = pltpu.make_async_remote_copy(
                src_ref=otm, dst_ref=otm_got, send_sem=send_sems.at[len(PLACE)],
                recv_sem=recv_sems.at[len(PLACE)], device_id={"mode": before}, device_id_type=MESH)
            otm_copy.start()

    def factor(otm_ref, picked, line):
        rows = wide[pl.ds(line, ATT, stride=LINES), :].astype(BF16)
        return lax.dot_general(
            otm_ref[...], rows, (((0,), (0,)), ((), ())), preferred_element_type=F32
        ).astype(BF16)

    def spectra(left, right):
        return lax.dot_general(left, right, (((1,), (1,)), ((), ())), preferred_element_type=F32) * (1.0 / 64.0)

    wide[...] = pick[...].astype(F32)
    crossing = []
    for line in range(LINES):
        here = factor(otm, pick, line)
        lane = lax.broadcasted_iota(jnp.int32, here.shape, 1)
        turned = pltpu.roll(here.astype(F32), 64, 1)
        turned = jnp.where(lane < 64, turned, -turned).astype(BF16)
        csd_ref[0, line, 0] = spectra(here, here).astype(BF16)
        csd_ref[0, line, 1] = spectra(turned, here).astype(BF16)
        crossing.append((here[:CROSS], turned[:CROSS]))
    otm_copy.wait_recv()
    for copy in tails:
        copy.wait_recv()
    wide[...] = jnp.where(me == NY * NZ - 1, 0.0, pick_got[...].astype(F32))
    for line in range(LINES):
        following = factor(otm_got, pick_got, line)
        here, turned = crossing[line]
        joint_ref[0, line, 0] = spectra(here, following).astype(BF16)
        joint_ref[0, line, 1] = spectra(turned, following).astype(BF16)
    for copy in (*copies.values(), otm_copy):
        copy.wait_send()


def per_device(mode_shapes, modal_freq, damping, excitation, modal_load, attach, row_count, otm):
    iface, modes = mode_shapes.shape
    rows_max, width = otm.shape[1], modal_load.shape[3]
    columns = LINES * 2 * width
    vmem = pl.BlockSpec(memory_space=pltpu.VMEM)
    hbm = pl.BlockSpec(memory_space=pltpu.HBM)
    smem = pl.BlockSpec(memory_space=pltpu.SMEM)
    operands = (
        modal_freq,
        damping,
        excitation,
        modal_load.transpose(1, 2, 3, 0).reshape(columns, modes),
        attach,
        row_count,
        otm[0].T,
        mode_shapes,
    )
    return tuple(
        pl.pallas_call(
            kernel,
            out_shape=[
                jax.ShapeDtypeStruct((1, LINES, 2, rows_max, rows_max), BF16),
                jax.ShapeDtypeStruct((1, LINES, 2, CROSS, rows_max), BF16),
            ],
            in_specs=[hbm] * 4 + [smem] * 2 + [hbm] * 2,
            out_specs=[vmem] * 2,
            scratch_shapes=[
                pltpu.VMEM((modes,), F32),
                pltpu.VMEM((modes,), F32),
                pltpu.SMEM((LINES,), F32),
                pltpu.VMEM((columns, modes), F32),
                pltpu.VMEM((ATT, rows_max), BF16),
                pltpu.VMEM((iface, modes), BF16),
                pltpu.VMEM((columns, modes), BF16),
                pltpu.VMEM((iface * LINES, 128), F32),
                pltpu.VMEM((2 * NZ * TALL, 128), F32),
                pltpu.VMEM((ATT * LINES, 128), F32),
                pltpu.VMEM((TOTAL, 128), BF16),
                pltpu.VMEM((TOTAL, 128), BF16),
                pltpu.VMEM((ATT, rows_max), BF16),
                pltpu.VMEM((ATT * LINES, 128), BF16),
                pltpu.VMEM((ATT * LINES, 128), BF16),
                pltpu.VMEM((ATT * LINES, 128), F32),
                pltpu.SemaphoreType.DMA((5 + PIECES,)),
                pltpu.SemaphoreType.DMA((SLOTS,)),
                pltpu.SemaphoreType.DMA((SLOTS,)),
            ],
            compiler_params=pltpu.CompilerParams(
                vmem_limit_bytes=42 << 20, collective_id=0, has_side_effects=True
            ),
            name="loads",
        )(*(value if value is row_count or value is attach else pltpu.with_memory_space_constraint(value, pltpu.HBM) for value in operands))
    )


def solution(mesh):
    return jax.shard_map(
        per_device,
        mesh=mesh,
        in_specs=(
            P(None, "mode"),
            P("mode"),
            P("mode"),
            P("freq"),
            P("mode", "freq", None, None),
            P(),
            P("mode"),
            P("mode", None, None),
        ),
        out_specs=(P("mode", "freq", None, None, None), P("mode", "freq", None, None, None)),
        check_vma=False,
    )
```

```python
import jax
import jax.numpy as jnp
from jax import lax
from jax.experimental import pallas as pl
from jax.experimental.pallas import tpu as pltpu
from jax.sharding import PartitionSpec as P

MESH = pl.DeviceIdType.MESH
F32, BF16 = jnp.float32, jnp.bfloat16
NY, NZ = 4, 8
SIZE = {"y": NY, "z": NZ}
OTHER = {"y": "z", "z": "y"}
COMPS, ATT, LINES, CROSS = 32, 96, 4, 128
PIECES = 4
CHUNKS = (
    ("z", 0, 16), ("z", 16, 16), ("y", 32, 12), ("y", 44, 28), ("y", 72, 24),
)
ORDER = (
    (0, 4), (1, 4), (2, 2), (3, 2), (4, 2), (0, 3), (1, 3), (2, 1), (3, 1), (0, 2), (4, 1), (1, 2), (2, 0),
    (0, 1), (1, 1), (3, 0), (2, -1), (0, 0), (1, 0), (4, 0), (0, -1), (1, -1), (3, -1), (4, -1),
)
TALL = max(rows for _, _, rows in CHUNKS) * LINES


def plan():
    place, total = {}, 0
    for index, (first, _, rows) in enumerate(CHUNKS):
        n, m, tall = SIZE[first], SIZE[OTHER[first]], rows * LINES
        for hop in range(n // 2, 0, -1):
            size = m * tall // (2 if hop == n // 2 else 1)
            for side in range(2):
                place[(index, hop, side)] = (len(place), total, size)
                total += size
        for step in range(1, m):
            place[(index, "direct", step)] = (len(place), total, tall)
            total += tall
    return place, total


PLACE, TOTAL = plan()
SLOTS = len(PLACE) + 1 + len(CHUNKS)


def kernel(freq_hbm, damp_hbm, exc_hbm, load_hbm, attach_hbm, count_hbm, otm_hbm, shapes_hbm, csd_ref, joint_ref,
           freq, damp, exc_smem, load, attach, count_smem, otm, shapes, resp, whole, own, mine, sent, got,
           otm_got, pick, pick_got, wide, in_sems, send_sems, recv_sems):
    me = lax.axis_index("mode")
    at = {"y": me // NZ, "z": lax.rem(me, NZ)}

    def device(axis, offset):
        if axis == "z":
            return at["y"] * NZ + lax.rem(at["z"] + offset + NZ, NZ)
        return lax.rem(at["y"] + offset + NY, NY) * NZ + at["z"]

    before = lax.rem(me + NY * NZ - 1, NY * NZ)
    after = lax.rem(me + 1, NY * NZ)
    small = [(freq_hbm, freq), (damp_hbm, damp), (exc_hbm, exc_smem), (load_hbm, load), (count_hbm, count_smem),
             (otm_hbm, otm), (attach_hbm, attach)]
    rows = shapes.shape[0] // PIECES
    parts = [pl.ds(piece * rows, rows) for piece in range(PIECES)]
    loads = [pltpu.make_async_copy(src, dst, in_sems.at[k]) for k, (src, dst) in enumerate(small)]
    loads += [
        pltpu.make_async_copy(shapes_hbm.at[part], shapes.at[part], in_sems.at[len(small) + k])
        for k, part in enumerate(parts)
    ]
    for copy in loads:
        copy.start()
    barrier = pltpu.get_barrier_semaphore()
    peers = [device("z", step) for step in range(1, NZ)] + [device("y", step) for step in range(1, NY)]
    for peer in (*peers, before, after):
        pl.semaphore_signal(barrier, inc=1, device_id={"mode": peer}, device_id_type=MESH)
    for copy in loads[:4]:
        copy.wait()
    omega = freq[...].reshape(1, -1)
    ratio = damp[...].reshape(1, -1)
    omega_sq = omega * omega
    for line in range(LINES):
        exc = exc_smem[line]
        a = omega_sq - exc * exc
        b = 2.0 * ratio * omega * exc
        denom = a * a + b * b
        frf_re = omega_sq * a / denom
        frf_im = -omega_sq * b / denom
        load_re = load[pl.ds(line * 128, 64), :]
        load_im = load[pl.ds(line * 128 + 64, 64), :]
        resp[pl.ds(line * 128, 64), :] = (frf_re * load_re - frf_im * load_im).astype(BF16)
        resp[pl.ds(line * 128 + 64, 64), :] = (frf_re * load_im + frf_im * load_re).astype(BF16)
    for piece in range(PIECES):
        loads[len(small) + piece].wait()
        block = lax.dot_general(
            shapes[parts[piece], :], resp[...], (((1,), (1,)), ((), ())), preferred_element_type=F32
        )
        for line in range(LINES):
            whole[pl.ds(piece * rows * LINES + line, rows, stride=LINES), :] = block[:, line * 128 : line * 128 + 128]
    for copy in loads[4:7]:
        copy.wait()
    keep = lax.broadcasted_iota(jnp.int32, otm.shape, 1) < count_smem[0]
    otm[...] = jnp.where(keep, otm[...].astype(F32), 0.0).astype(BF16)

    pl.semaphore_wait(barrier, len(peers) + 2)
    copies, tails = {}, []
    table = whole.reshape(whole.shape[0] // LINES, LINES, 128)

    def send(key, place, target, source=sent, dest=got):
        number, offset, size = place
        part = pl.ds(offset, size)
        copy = pltpu.make_async_remote_copy(
            src_ref=source.at[part], dst_ref=dest.at[part], send_sem=send_sems.at[number],
            recv_sem=recv_sems.at[number], device_id={"mode": target}, device_id_type=MESH)
        copy.start()
        copies[key] = copy
        return copy

    def event(index, hop):
        first, start, rows = CHUNKS[index]
        other = OTHER[first]
        n, m, tall = SIZE[first], SIZE[other], rows * LINES

        def block(offset, item):
            return pl.ds(pl.multiple_of(offset + item * tall, 16), tall)

        def gather(dest, item, slot):
            unit = item * NZ + dest if first == "z" else dest * NZ + item
            base = pl.multiple_of(slot * tall, 16)
            for row in range(rows):
                source = attach[unit, start + row]
                own[pl.ds(base + row * LINES, LINES), :] = table[source]

        if hop > 0:
            half = m // 2
            dests = [lax.rem(at[first] + (hop if side == 0 else n - hop), n) for side in range(2)]

            def fetch(low, high):
                def body(item, carry):
                    for side in range(2):
                        gather(dests[side], item + side * low, side * m + item + side * low)
                    return carry

                lax.fori_loop(0, high, body, 0)

            if hop == n // 2:
                fetch(half, half)
            else:
                fetch(0, m)
            for side in range(2):
                place = PLACE[(index, hop, side)]
                if hop == n // 2:
                    def fill(item, carry):
                        sent[block(place[1], item), :] = own[block(0, side * (m + half) + item), :].astype(BF16)
                        return carry

                    lax.fori_loop(0, half, fill, 0)
                else:
                    copies[(index, hop + 1, side)].wait_recv()
                    arrived = PLACE[(index, hop + 1, side)][1]
                    short = hop + 1 == n // 2
                    skip = side * half if short else 0

                    def fill(item, carry):
                        value = own[block(0, side * m + skip + item), :] + got[block(arrived, item), :].astype(F32)
                        sent[block(place[1], skip + item), :] = value.astype(BF16)
                        if short:
                            rest = (1 - side) * half + item
                            sent[block(place[1], rest), :] = own[block(0, side * m + rest), :].astype(BF16)
                        return carry

                    lax.fori_loop(0, half if short else m, fill, 0)
                send((index, hop, side), place, device(first, 1 if side == 0 else -1))
        elif hop == 0:
            def body(item, carry):
                gather(at[first], item, item)
                return carry

            lax.fori_loop(0, m, body, 0)
            arrived = [PLACE[(index, 1, side)][1] for side in range(2)]
            for side in range(2):
                copies[(index, 1, side)].wait_recv()

            def value(item):
                here = own[block(0, item), :]
                for side in range(2):
                    here = here + got[block(arrived[side], item), :].astype(F32)
                return here

            for step in sorted(range(1, m), key=lambda step: -min(step, m - step)):
                place = PLACE[(index, "direct", step)]
                sent[pl.ds(place[1], tall), :] = value(lax.rem(at[other] + step, m)).astype(BF16)
                send((index, "direct", step), place, device(other, step))
            mine[pl.ds(start * LINES, tall), :] = value(at[other])
        else:
            here = mine[pl.ds(start * LINES, tall), :]
            for step in range(1, m):
                copies[(index, "direct", step)].wait_recv()
                here = here + got[pl.ds(PLACE[(index, "direct", step)][1], tall), :].astype(F32)
            pick[pl.ds(start * LINES, tall), :] = here.astype(BF16)
            place = (len(PLACE) + 1 + index, start * LINES, tall)
            tails.append(send((index, "pick"), place, before, pick, pick_got))

    for number, (index, hop) in enumerate(ORDER):
        event(index, hop)
        if number == 4:
            otm_copy = pltpu.make_async_remote_copy(
                src_ref=otm, dst_ref=otm_got, send_sem=send_sems.at[len(PLACE)],
                recv_sem=recv_sems.at[len(PLACE)], device_id={"mode": before}, device_id_type=MESH)
            otm_copy.start()

    def factor(otm_ref, picked, line):
        rows = wide[pl.ds(line, ATT, stride=LINES), :].astype(BF16)
        return lax.dot_general(
            otm_ref[...], rows, (((0,), (0,)), ((), ())), preferred_element_type=F32
        ).astype(BF16)

    def spectra(left, right):
        return lax.dot_general(left, right, (((1,), (1,)), ((), ())), preferred_element_type=F32) * (1.0 / 64.0)

    wide[...] = pick[...].astype(F32)
    crossing = []
    for line in range(LINES):
        here = factor(otm, pick, line)
        lane = lax.broadcasted_iota(jnp.int32, here.shape, 1)
        turned = pltpu.roll(here.astype(F32), 64, 1)
        turned = jnp.where(lane < 64, turned, -turned).astype(BF16)
        csd_ref[0, line, 0] = spectra(here, here).astype(BF16)
        csd_ref[0, line, 1] = spectra(turned, here).astype(BF16)
        crossing.append((here[:CROSS], turned[:CROSS]))
    otm_copy.wait_recv()
    for copy in tails:
        copy.wait_recv()
    wide[...] = jnp.where(me == NY * NZ - 1, 0.0, pick_got[...].astype(F32))
    for line in range(LINES):
        following = factor(otm_got, pick_got, line)
        here, turned = crossing[line]
        joint_ref[0, line, 0] = spectra(here, following).astype(BF16)
        joint_ref[0, line, 1] = spectra(turned, following).astype(BF16)
    for copy in (*copies.values(), otm_copy):
        copy.wait_send()


def store(csd_ref, joint_ref, csd_hbm, joint_hbm, sems):
    copies = []
    for line in range(LINES):
        copies.append(pltpu.make_async_copy(csd_ref.at[0, line], csd_hbm.at[0, line], sems.at[2 * line]))
        copies.append(pltpu.make_async_copy(joint_ref.at[0, line], joint_hbm.at[0, line], sems.at[2 * line + 1]))
    for copy in copies:
        copy.start()
    for copy in copies:
        copy.wait()


def per_device(mode_shapes, modal_freq, damping, excitation, modal_load, attach, row_count, otm):
    iface, modes = mode_shapes.shape
    rows_max, width = otm.shape[1], modal_load.shape[3]
    columns = LINES * 2 * width
    vmem = pl.BlockSpec(memory_space=pltpu.VMEM)
    hbm = pl.BlockSpec(memory_space=pltpu.HBM)
    operands = (
        modal_freq,
        damping,
        excitation,
        modal_load.transpose(1, 2, 3, 0).reshape(columns, modes),
        attach,
        row_count,
        otm[0].T,
        mode_shapes,
    )
    spectra = pl.pallas_call(
            kernel,
            out_shape=[
                jax.ShapeDtypeStruct((1, LINES, 2, rows_max, rows_max), BF16),
                jax.ShapeDtypeStruct((1, LINES, 2, CROSS, rows_max), BF16),
            ],
            in_specs=[hbm] * 8,
            out_specs=[vmem] * 2,
            scratch_shapes=[
                pltpu.VMEM((modes,), F32),
                pltpu.VMEM((modes,), F32),
                pltpu.SMEM((LINES,), F32),
                pltpu.VMEM((columns, modes), F32),
                pltpu.SMEM((COMPS, ATT), jnp.int32),
                pltpu.SMEM((1,), jnp.int32),
                pltpu.VMEM((ATT, rows_max), BF16),
                pltpu.VMEM((iface, modes), BF16),
                pltpu.VMEM((columns, modes), BF16),
                pltpu.VMEM((iface * LINES, 128), F32),
                pltpu.VMEM((2 * NZ * TALL, 128), F32),
                pltpu.VMEM((ATT * LINES, 128), F32),
                pltpu.VMEM((TOTAL, 128), BF16),
                pltpu.VMEM((TOTAL, 128), BF16),
                pltpu.VMEM((ATT, rows_max), BF16),
                pltpu.VMEM((ATT * LINES, 128), BF16),
                pltpu.VMEM((ATT * LINES, 128), BF16),
                pltpu.VMEM((ATT * LINES, 128), F32),
                pltpu.SemaphoreType.DMA((7 + PIECES,)),
                pltpu.SemaphoreType.DMA((SLOTS,)),
                pltpu.SemaphoreType.DMA((SLOTS,)),
            ],
            compiler_params=pltpu.CompilerParams(
                vmem_limit_bytes=42 << 20, collective_id=0, has_side_effects=True
            ),
            name="loads",
        )(*(value if value is row_count else pltpu.with_memory_space_constraint(value, pltpu.HBM) for value in operands))
    return tuple(
        pl.pallas_call(
            store,
            out_shape=[jax.ShapeDtypeStruct(value.shape, BF16) for value in spectra],
            in_specs=[vmem] * 2,
            out_specs=[hbm] * 2,
            scratch_shapes=[pltpu.SemaphoreType.DMA((2 * LINES,))],
            compiler_params=pltpu.CompilerParams(vmem_limit_bytes=1 << 20),
            name="store",
        )(*spectra)
    )


def solution(mesh):
    return jax.shard_map(
        per_device,
        mesh=mesh,
        in_specs=(
            P(None, "mode"),
            P("mode"),
            P("mode"),
            P("freq"),
            P("mode", "freq", None, None),
            P(),
            P("mode"),
            P("mode", None, None),
        ),
        out_specs=(P("mode", "freq", None, None, None), P("mode", "freq", None, None, None)),
        check_vma=False,
    )
```

```python
import jax
import jax.numpy as jnp
from jax import lax
from jax.experimental import pallas as pl
from jax.experimental.pallas import tpu as pltpu
from jax.sharding import PartitionSpec as P

MESH = pl.DeviceIdType.MESH
F32, BF16 = jnp.float32, jnp.bfloat16
NY, NZ = 4, 8
SIZE = {"y": NY, "z": NZ}
OTHER = {"y": "z", "z": "y"}
COMPS, ATT, LINES, CROSS = 32, 96, 4, 128
PIECES = 4
WAYS = {
    ("z", 4): (((4, 3),), ((3, 2),), ((2, 1),), ((1, 0),)),
    ("z", 3): (((4, 2), (3, 2)), ((2, 1),), ((1, 0),)),
    ("z", 2): (((4, 2), (3, 2), (1, 0)), ((2, 0),)),
    ("z", 1): (((4, 0), (3, 0), (2, 0), (1, 0)),),
    ("y", 2): (((2, 1),), ((1, 0),)),
    ("y", 1): (((2, 0), (1, 0)),),
}
CHUNKS = (
    ("y", 2, 3, 0, 0, 16), ("z", 3, 1, 0, 16, 16), ("y", 2, 2, 0, 32, 8), ("y", 2, 2, 0, 40, 16),
    ("y", 2, 1, 0, 56, 16), ("z", 3, 1, 0, 72, 16), ("z", 3, 1, 0, 88, 8),
)
ORDER = (
    (0, 3, 0), (0, 0, 0), (1, 3, 0), (1, 0, 0), (2, 3, 0), (2, 0, 0), (3, 3, 0), (3, 0, 0), (4, 3, 0),
    (4, 0, 0), (5, 3, 0), (5, 0, 0), (6, 3, 0), (6, 0, 0), (-1, 0, 2), (0, 3, 1), (0, 0, 1), (2, 3, 1),
    (2, 0, 1), (1, 3, 1), (3, 3, 1), (1, 0, 1), (3, 0, 1), (4, 3, 1), (5, 3, 1), (4, 0, 1), (6, 3, 1),
    (0, 3, -1), (1, 3, 2), (2, 3, -1), (3, 3, -1), (5, 0, 1), (5, 3, 2), (4, 3, -1), (6, 3, 2), (6, 3, -1),
    (1, 3, -1), (5, 3, -1), (6, 0, 1), (0, 1, 0), (1, 0, 2), (2, 1, 0), (5, 0, 2), (6, 0, 2), (3, 1, 0),
    (0, 1, 1), (1, 1, 0), (2, 1, 1), (4, 1, 0), (5, 1, 0), (6, 1, 0), (3, 1, 1), (0, 1, 2), (1, 2, 0),
    (2, 2, 0), (5, 2, 0), (6, 2, 0), (4, 2, 0), (0, 2, 0), (3, 2, 0),
)
PAIR = 4
TALL = max(chunk[-1] for chunk in CHUNKS) * PAIR


def axes(index):
    first, way, other_way = CHUNKS[index][:3]
    return ((first, way), (OTHER[first], other_way))


def both_ways(index, stage, k):
    opposite = 2 * k == SIZE[axes(index)[stage][0]]
    return (index % 2,) if stage == 1 and opposite else (0, 1)


def plan():
    place, total = {}, 0
    for index, chunk in enumerate(CHUNKS):
        tall = chunk[-1] * PAIR
        for stage, way in enumerate(axes(index)):
            for k, j in (copy for turn in WAYS[way] for copy in turn):
                size = tall
                if stage == 0:
                    size *= SIZE[OTHER[way[0]]]
                    size //= 2 if 2 * k == SIZE[way[0]] else 1
                for side in both_ways(index, stage, k):
                    place[(index, stage, k, j, side)] = (len(place), total, size)
                    total += size
    return place, total


PLACE, TOTAL = plan()
OWN = [sum(chunk[-1] for chunk in CHUNKS[:index]) * PAIR * COMPS for index in range(len(CHUNKS))]
SLOTS = len(PLACE) + 1 + len(CHUNKS)


def kernel(freq_hbm, damp_hbm, exc_hbm, load_hbm, attach_hbm, count_hbm, otm_hbm, shapes_hbm, csd_ref, joint_ref,
           freq, damp, exc_smem, load, attach, count_smem, otm, shapes, resp, whole, own, held, mine, sent, got,
           otm_got, pick, pick_got, wide, crossing, in_sems, send_sems, recv_sems):
    me = lax.axis_index("mode")
    at = {"y": me // NZ, "z": lax.rem(me, NZ)}

    def device(axis, offset):
        if axis == "z":
            return at["y"] * NZ + lax.rem(at["z"] + offset + NZ, NZ)
        return lax.rem(at["y"] + offset + NY, NY) * NZ + at["z"]

    before = lax.rem(me + NY * NZ - 1, NY * NZ)
    after = lax.rem(me + 1, NY * NZ)
    rows = shapes.shape[0] // PIECES
    parts = [pl.ds(piece * rows, rows) for piece in range(PIECES)]
    halves = [pl.ds(pair * PAIR * 128, PAIR * 128) for pair in range(LINES // PAIR)]
    moves = [(freq_hbm, freq), (damp_hbm, damp), (exc_hbm, exc_smem), (load_hbm.at[halves[0]], load.at[halves[0]])]
    moves += [(shapes_hbm.at[part], shapes.at[part]) for part in parts]
    moves += [(attach_hbm, attach), (otm_hbm, otm), (count_hbm, count_smem)]
    moves += [(load_hbm.at[half], load.at[half]) for half in halves[1:]]
    loads = [pltpu.make_async_copy(src, dst, in_sems.at[k]) for k, (src, dst) in enumerate(moves)]
    for copy in loads:
        copy.start()
    barrier = pltpu.get_barrier_semaphore()
    peers = [device("z", step) for step in range(1, NZ)] + [device("y", step) for step in range(1, NY)]
    for peer in (*peers, before, after):
        pl.semaphore_signal(barrier, inc=1, device_id={"mode": peer}, device_id_type=MESH)
    for copy in loads[:4]:
        copy.wait()
    omega = freq[...].reshape(1, -1)
    ratio = damp[...].reshape(1, -1)
    omega_sq = omega * omega

    def products(pair):
        for line in range(pair * PAIR, pair * PAIR + PAIR):
            exc = exc_smem[line]
            a = omega_sq - exc * exc
            b = 2.0 * ratio * omega * exc
            denom = a * a + b * b
            frf_re = omega_sq * a / denom
            frf_im = -omega_sq * b / denom
            load_re = load[pl.ds(line * 128, 64), :]
            load_im = load[pl.ds(line * 128 + 64, 64), :]
            resp[pl.ds(line * 128, 64), :] = (frf_re * load_re - frf_im * load_im).astype(BF16)
            resp[pl.ds(line * 128 + 64, 64), :] = (frf_re * load_im + frf_im * load_re).astype(BF16)
        for piece in range(PIECES):
            if pair == 0:
                loads[4 + piece].wait()
            block = lax.dot_general(
                shapes[parts[piece], :], resp[halves[pair], :], (((1,), (1,)), ((), ())), preferred_element_type=F32
            )
            for side in range(PAIR):
                place = pl.ds(piece * rows * LINES + pair * PAIR + side, rows, stride=LINES)
                whole[place, :] = block[:, side * 128 : side * 128 + 128]

    products(0)
    loads[4 + PIECES].wait()
    pl.semaphore_wait(barrier, len(peers) + 2)
    copies, tails = {}, [[] for _ in range(LINES // PAIR)]
    table = whole.reshape(whole.shape[0] // LINES, LINES, 128)

    def send(key, place, target, source=sent, dest=got):
        number, offset, size = place
        part = pl.ds(offset, size)
        copy = pltpu.make_async_remote_copy(
            src_ref=source.at[part], dst_ref=dest.at[part], send_sem=send_sems.at[number],
            recv_sem=recv_sems.at[number], device_id={"mode": target}, device_id_type=MESH)
        copy.start()
        copies[key] = copy
        return copy

    def event(index, stage, turn):
        pair, start, rows = CHUNKS[index][3:]
        (first, way), (other, other_way) = axes(index)
        n, m, tall = SIZE[first], SIZE[other], rows * PAIR
        half = m // 2
        home = pl.ds(pair * ATT * PAIR + start * PAIR, tall)

        def block(offset, item):
            return pl.ds(pl.multiple_of(offset + item * tall, 16), tall)

        def gather(dest, item, base):
            unit = item * NZ + dest if first == "z" else dest * NZ + item
            for row in range(rows):
                source = attach[unit, start + row]
                own[pl.ds(base + row * PAIR, PAIR), :] = table[source, pl.ds(pair * PAIR, PAIR), :]

        def arrivals(which, k, side):
            found = [
                (index, which, source, k, side)
                for step in WAYS[axes(index)[which]]
                for source, target in step
                if target == k and side in both_ways(index, which, source)
            ]
            for key in found:
                copies[key].wait_recv()
            return found

        def region(k, side):
            return OWN[index] + (k if side == 0 else (n - k) % n) * m * tall

        if stage == 3:
            kept = [(0, 0, m, 0)]
            for k, side, count, skip in kept if turn < 0 else [
                (k, side, *((half, side * half) if 2 * k == n else (m, 0)))
                for k, _ in WAYS[first, way][turn]
                for side in range(2)
            ]:
                dest = lax.rem(at[first] + (k if side == 0 else n - k), n)

                def body(item, carry):
                    gather(dest, item + skip, pl.multiple_of(region(k, side) + (item + skip) * tall, 16))
                    return carry

                lax.fori_loop(0, count, body, 0)
        elif stage == 0:
            for k, j, side in ((k, j, side) for k, j in WAYS[first, way][turn] for side in range(2)):
                count, skip = (half, side * half) if 2 * k == n else (m, 0)
                place = PLACE[(index, 0, k, j, side)]
                found = arrivals(0, k, side)
                short = [PLACE[key][1] for key in found if 2 * key[2] == n]
                full = [PLACE[key][1] for key in found if 2 * key[2] != n]

                def put(item, partly):
                    value = own[block(region(k, side), item + skip), :]
                    for offset in full:
                        value = value + got[block(offset, item), :].astype(F32)
                    for offset in short if partly is not None else ():
                        value = value + got[block(offset, partly), :].astype(F32)
                    sent[block(place[1], item), :] = value.astype(BF16)

                if short:
                    def fill(item, carry):
                        put(side * half + item, item)
                        put((1 - side) * half + item, None)
                        return carry

                    lax.fori_loop(0, half, fill, 0)
                else:
                    def fill(item, carry):
                        put(item, None)
                        return carry

                    lax.fori_loop(0, count, fill, 0)
                send((index, 0, k, j, side), place, device(first, k - j if side == 0 else j - k))
        elif stage == 1 and turn == 0:
            arrived = [PLACE[key][1] for side in range(2) for key in arrivals(0, 0, side)]

            def value(item):
                here = own[block(region(0, 0), item), :]
                for offset in arrived:
                    here = here + got[block(offset, item), :].astype(F32)
                return here

            targets = dict(WAYS[other, other_way][0])
            for k in (*sorted(targets, reverse=True), *(k for k in range(1, half + 1) if k not in targets)):
                for side in both_ways(index, 1, k):
                    here = value(lax.rem(at[other] + (k if side == 0 else m - k), m))
                    if k in targets:
                        j = targets[k]
                        place = PLACE[(index, 1, k, j, side)]
                        sent[pl.ds(place[1], tall), :] = here.astype(BF16)
                        send((index, 1, k, j, side), place, device(other, k - j if side == 0 else j - k))
                    else:
                        held[pl.ds(((index * half + k - 1) * 2 + side) * TALL, tall), :] = here
            mine[home, :] = value(at[other])
        elif stage == 1:
            for k, j in WAYS[other, other_way][turn]:
                for side in both_ways(index, 1, k):
                    here = held[pl.ds(((index * half + k - 1) * 2 + side) * TALL, tall), :]
                    for key in arrivals(1, k, side):
                        here = here + got[pl.ds(PLACE[key][1], tall), :].astype(F32)
                    place = PLACE[(index, 1, k, j, side)]
                    sent[pl.ds(place[1], tall), :] = here.astype(BF16)
                    send((index, 1, k, j, side), place, device(other, k - j if side == 0 else j - k))
        else:
            here = mine[home, :]
            for side in range(2):
                for key in arrivals(1, 0, side):
                    here = here + got[pl.ds(PLACE[key][1], tall), :].astype(F32)
            pick[home, :] = here.astype(BF16)
            place = (len(PLACE) + 1 + index, pair * ATT * PAIR + start * PAIR, tall)
            tails[pair].append(send((index, "pick"), place, before, pick, pick_got))

    def factor(otm_ref, side):
        picked = wide[pl.ds(side, ATT, stride=PAIR), :].astype(BF16)
        return lax.dot_general(
            otm_ref[...], picked, (((0,), (0,)), ((), ())), preferred_element_type=F32
        ).astype(BF16)

    def spectra(left, right):
        return lax.dot_general(left, right, (((1,), (1,)), ((), ())), preferred_element_type=F32) * (1.0 / 64.0)

    def direct(pair):
        wide[...] = pick[pl.ds(pair * ATT * PAIR, ATT * PAIR), :].astype(F32)
        for side in range(PAIR):
            line = pair * PAIR + side
            here = factor(otm, side)
            lane = lax.broadcasted_iota(jnp.int32, here.shape, 1)
            turned = pltpu.roll(here.astype(F32), 64, 1)
            turned = jnp.where(lane < 64, turned, -turned).astype(BF16)
            csd_ref[0, line, 0] = spectra(here, here).astype(BF16)
            csd_ref[0, line, 1] = spectra(turned, here).astype(BF16)
            crossing[line, 0] = here[:CROSS]
            crossing[line, 1] = turned[:CROSS]

    def joint(pair):
        for copy in tails[pair]:
            copy.wait_recv()
        arrived = pick_got[pl.ds(pair * ATT * PAIR, ATT * PAIR), :].astype(F32)
        wide[...] = jnp.where(me == NY * NZ - 1, 0.0, arrived)
        for side in range(PAIR):
            line = pair * PAIR + side
            following = factor(otm_got, side)
            for part in range(2):
                joint_ref[0, line, part] = spectra(crossing[line, part], following).astype(BF16)

    for index, stage, turn in ORDER:
        if index >= 0:
            event(index, stage, turn)
        elif turn == 0:
            loads[7 + PIECES].wait()
            products(1)
        elif turn == 1:
            direct(0)
        else:
            loads[5 + PIECES].wait()
            loads[6 + PIECES].wait()
            keep = lax.broadcasted_iota(jnp.int32, otm.shape, 1) < count_smem[0]
            otm[...] = jnp.where(keep, otm[...].astype(F32), 0.0).astype(BF16)
            otm_copy = pltpu.make_async_remote_copy(
                src_ref=otm, dst_ref=otm_got, send_sem=send_sems.at[len(PLACE)],
                recv_sem=recv_sems.at[len(PLACE)], device_id={"mode": before}, device_id_type=MESH)
            otm_copy.start()
    direct(LINES // PAIR - 1)
    otm_copy.wait_recv()
    for pair in range(LINES // PAIR):
        joint(pair)
    for copy in (*copies.values(), otm_copy):
        copy.wait_send()


def store(csd_ref, joint_ref, csd_hbm, joint_hbm, sems):
    copies = []
    for line in range(LINES):
        copies.append(pltpu.make_async_copy(csd_ref.at[0, line], csd_hbm.at[0, line], sems.at[2 * line]))
        copies.append(pltpu.make_async_copy(joint_ref.at[0, line], joint_hbm.at[0, line], sems.at[2 * line + 1]))
    for copy in copies:
        copy.start()
    for copy in copies:
        copy.wait()


def per_device(mode_shapes, modal_freq, damping, excitation, modal_load, attach, row_count, otm):
    iface, modes = mode_shapes.shape
    rows_max, width = otm.shape[1], modal_load.shape[3]
    columns = LINES * 2 * width
    vmem = pl.BlockSpec(memory_space=pltpu.VMEM)
    hbm = pl.BlockSpec(memory_space=pltpu.HBM)
    operands = (
        modal_freq,
        damping,
        excitation,
        modal_load.transpose(1, 2, 3, 0).reshape(columns, modes),
        attach,
        row_count,
        otm[0].T,
        mode_shapes,
    )
    spectra = pl.pallas_call(
            kernel,
            out_shape=[
                jax.ShapeDtypeStruct((1, LINES, 2, rows_max, rows_max), BF16),
                jax.ShapeDtypeStruct((1, LINES, 2, CROSS, rows_max), BF16),
            ],
            in_specs=[hbm] * 8,
            out_specs=[vmem] * 2,
            scratch_shapes=[
                pltpu.VMEM((modes,), F32),
                pltpu.VMEM((modes,), F32),
                pltpu.SMEM((LINES,), F32),
                pltpu.VMEM((columns, modes), F32),
                pltpu.SMEM((COMPS, ATT), jnp.int32),
                pltpu.SMEM((1,), jnp.int32),
                pltpu.VMEM((ATT, rows_max), BF16),
                pltpu.VMEM((iface, modes), BF16),
                pltpu.VMEM((columns, modes), BF16),
                pltpu.VMEM((iface * LINES, 128), F32),
                pltpu.VMEM((COMPS * ATT * LINES, 128), F32),
                pltpu.VMEM((len(CHUNKS) * NZ * TALL, 128), F32),
                pltpu.VMEM((ATT * LINES, 128), F32),
                pltpu.VMEM((TOTAL, 128), BF16),
                pltpu.VMEM((TOTAL, 128), BF16),
                pltpu.VMEM((ATT, rows_max), BF16),
                pltpu.VMEM((ATT * LINES, 128), BF16),
                pltpu.VMEM((ATT * LINES, 128), BF16),
                pltpu.VMEM((ATT * PAIR, 128), F32),
                pltpu.VMEM((LINES, 2, CROSS, 128), BF16),
                pltpu.SemaphoreType.DMA((8 + PIECES,)),
                pltpu.SemaphoreType.DMA((SLOTS,)),
                pltpu.SemaphoreType.DMA((SLOTS,)),
            ],
            compiler_params=pltpu.CompilerParams(
                vmem_limit_bytes=42 << 20, collective_id=0, has_side_effects=True
            ),
            name="loads",
        )(*(value if value is row_count else pltpu.with_memory_space_constraint(value, pltpu.HBM) for value in operands))
    return tuple(
        pl.pallas_call(
            store,
            out_shape=[jax.ShapeDtypeStruct(value.shape, BF16) for value in spectra],
            in_specs=[vmem] * 2,
            out_specs=[hbm] * 2,
            scratch_shapes=[pltpu.SemaphoreType.DMA((2 * LINES,))],
            compiler_params=pltpu.CompilerParams(vmem_limit_bytes=1 << 20),
            name="store",
        )(*spectra)
    )


def solution(mesh):
    return jax.shard_map(
        per_device,
        mesh=mesh,
        in_specs=(
            P(None, "mode"),
            P("mode"),
            P("mode"),
            P("freq"),
            P("mode", "freq", None, None),
            P(),
            P("mode"),
            P("mode", None, None),
        ),
        out_specs=(P("mode", "freq", None, None, None), P("mode", "freq", None, None, None)),
        check_vma=False,
    )
```

```python
import jax
import jax.numpy as jnp
from jax import lax
from jax.experimental import pallas as pl
from jax.experimental.pallas import tpu as pltpu
from jax.sharding import PartitionSpec as P

MESH = pl.DeviceIdType.MESH
F32, BF16 = jnp.float32, jnp.bfloat16
NY, NZ = 4, 8
SIZE = {"y": NY, "z": NZ}
OTHER = {"y": "z", "z": "y"}
COMPS, ATT, LINES, CROSS = 32, 96, 4, 128
CUTS = (0, 768, 2304, 4224, 6144)
PIECES = len(CUTS) - 1
WAYS = {
    ("z", 4): (((4, 3),), ((3, 2),), ((2, 1),), ((1, 0),)),
    ("z", 3): (((4, 2), (3, 2)), ((2, 1),), ((1, 0),)),
    ("z", 2): (((4, 2), (3, 2), (1, 0)), ((2, 0),)),
    ("z", 1): (((4, 0), (3, 0), (2, 0), (1, 0)),),
    ("y", 2): (((2, 1),), ((1, 0),)),
    ("y", 1): (((2, 0), (1, 0)),),
}
CHUNKS = (
    ("y", 2, 3, 0, 0, 16), ("z", 3, 1, 0, 16, 16), ("y", 2, 2, 0, 32, 8), ("y", 2, 2, 0, 40, 16),
    ("y", 2, 1, 0, 56, 16), ("z", 3, 1, 0, 72, 16), ("z", 3, 1, 0, 88, 8),
)
ORDER = (
    (0, 3, 0), (0, 0, 0), (1, 3, 0), (1, 0, 0), (2, 3, 0), (2, 0, 0), (3, 3, 0), (3, 0, 0), (4, 3, 0),
    (4, 0, 0), (5, 3, 0), (5, 0, 0), (6, 3, 0), (6, 0, 0), (-1, 0, 2), (0, 3, 1), (0, 0, 1), (2, 3, 1),
    (2, 0, 1), (1, 3, 1), (3, 3, 1), (1, 0, 1), (3, 0, 1), (4, 3, 1), (5, 3, 1), (4, 0, 1), (6, 3, 1),
    (0, 3, -1), (1, 3, 2), (2, 3, -1), (3, 3, -1), (5, 0, 1), (5, 3, 2), (4, 3, -1), (6, 3, 2), (6, 3, -1),
    (1, 3, -1), (5, 3, -1), (6, 0, 1), (0, 1, 0), (1, 0, 2), (2, 1, 0), (5, 0, 2), (6, 0, 2), (3, 1, 0),
    (0, 1, 1), (1, 1, 0), (2, 1, 1), (4, 1, 0), (5, 1, 0), (6, 1, 0), (3, 1, 1), (0, 1, 2), (1, 2, 0),
    (2, 2, 0), (5, 2, 0), (6, 2, 0), (4, 2, 0), (0, 2, 0), (3, 2, 0),
)
PAIR = 4
TALL = max(chunk[-1] for chunk in CHUNKS) * PAIR


def axes(index):
    first, way, other_way = CHUNKS[index][:3]
    return ((first, way), (OTHER[first], other_way))


def both_ways(index, stage, k):
    opposite = 2 * k == SIZE[axes(index)[stage][0]]
    return (index % 2,) if stage == 1 and opposite else (0, 1)


def plan():
    place, total = {}, 0
    for index, chunk in enumerate(CHUNKS):
        tall = chunk[-1] * PAIR
        for stage, way in enumerate(axes(index)):
            for k, j in (copy for turn in WAYS[way] for copy in turn):
                size = tall
                if stage == 0:
                    size *= SIZE[OTHER[way[0]]]
                    size //= 2 if 2 * k == SIZE[way[0]] else 1
                for side in both_ways(index, stage, k):
                    place[(index, stage, k, j, side)] = (len(place), total, size)
                    total += size
    return place, total


PLACE, TOTAL = plan()
OWN = [sum(chunk[-1] for chunk in CHUNKS[:index]) * PAIR * COMPS for index in range(len(CHUNKS))]
SLOTS = len(PLACE) + 1 + len(CHUNKS)


def kernel(freq_hbm, damp_hbm, exc_hbm, load_hbm, attach_hbm, count_hbm, otm_hbm, shapes_hbm, csd_ref, joint_ref,
           freq, damp, exc_smem, load, attach, count_smem, otm, shapes, resp, whole, own, held, mine, sent, got,
           otm_got, pick, pick_got, wide, crossing, in_sems, send_sems, recv_sems):
    me = lax.axis_index("mode")
    at = {"y": me // NZ, "z": lax.rem(me, NZ)}

    def device(axis, offset):
        if axis == "z":
            return at["y"] * NZ + lax.rem(at["z"] + offset + NZ, NZ)
        return lax.rem(at["y"] + offset + NY, NY) * NZ + at["z"]

    before = lax.rem(me + NY * NZ - 1, NY * NZ)
    after = lax.rem(me + 1, NY * NZ)
    parts = [pl.ds(low, high - low) for low, high in zip(CUTS, CUTS[1:])]
    halves = [pl.ds(pair * PAIR * 128, PAIR * 128) for pair in range(LINES // PAIR)]
    moves = [(freq_hbm, freq), (damp_hbm, damp), (exc_hbm, exc_smem), (load_hbm.at[halves[0]], load.at[halves[0]])]
    moves += [(shapes_hbm.at[part], shapes.at[part]) for part in parts]
    moves += [(attach_hbm, attach), (otm_hbm, otm), (count_hbm, count_smem)]
    moves += [(load_hbm.at[half], load.at[half]) for half in halves[1:]]
    loads = [pltpu.make_async_copy(src, dst, in_sems.at[k]) for k, (src, dst) in enumerate(moves)]
    for copy in loads:
        copy.start()
    barrier = pltpu.get_barrier_semaphore()
    peers = [device("z", step) for step in range(1, NZ)] + [device("y", step) for step in range(1, NY)]
    for peer in (*peers, before, after):
        pl.semaphore_signal(barrier, inc=1, device_id={"mode": peer}, device_id_type=MESH)
    for copy in loads[:4]:
        copy.wait()
    omega = freq[...].reshape(1, -1)
    ratio = damp[...].reshape(1, -1)
    omega_sq = omega * omega

    def products(pair):
        for line in range(pair * PAIR, pair * PAIR + PAIR):
            exc = exc_smem[line]
            a = omega_sq - exc * exc
            b = 2.0 * ratio * omega * exc
            denom = a * a + b * b
            frf_re = omega_sq * a / denom
            frf_im = -omega_sq * b / denom
            load_re = load[pl.ds(line * 128, 64), :]
            load_im = load[pl.ds(line * 128 + 64, 64), :]
            parted = [frf_re * load_re - frf_im * load_im, frf_re * load_im + frf_im * load_re]
            resp[:, pl.ds(line * 128, 128)] = jnp.concatenate(parted, axis=0).astype(BF16).T
        for piece in range(PIECES):
            if pair == 0:
                loads[4 + piece].wait()
            block = lax.dot_general(
                shapes[parts[piece], :], resp[:, halves[pair]], (((1,), (0,)), ((), ())), preferred_element_type=F32
            )
            for side in range(PAIR):
                place = pl.ds(CUTS[piece] * LINES + pair * PAIR + side, CUTS[piece + 1] - CUTS[piece], stride=LINES)
                whole[place, :] = block[:, side * 128 : side * 128 + 128]

    products(0)
    loads[4 + PIECES].wait()
    pl.semaphore_wait(barrier, len(peers) + 2)
    copies, tails = {}, [[] for _ in range(LINES // PAIR)]
    table = whole.reshape(whole.shape[0] // LINES, LINES, 128)

    def send(key, place, target, source=sent, dest=got):
        number, offset, size = place
        part = pl.ds(offset, size)
        copy = pltpu.make_async_remote_copy(
            src_ref=source.at[part], dst_ref=dest.at[part], send_sem=send_sems.at[number],
            recv_sem=recv_sems.at[number], device_id={"mode": target}, device_id_type=MESH)
        copy.start()
        copies[key] = copy
        return copy

    def event(index, stage, turn):
        pair, start, rows = CHUNKS[index][3:]
        (first, way), (other, other_way) = axes(index)
        n, m, tall = SIZE[first], SIZE[other], rows * PAIR
        half = m // 2
        home = pl.ds(pair * ATT * PAIR + start * PAIR, tall)

        def block(offset, item):
            return pl.ds(pl.multiple_of(offset + item * tall, 16), tall)

        def gather(dest, item, base):
            unit = item * NZ + dest if first == "z" else dest * NZ + item
            for row in range(rows):
                source = attach[unit, start + row]
                own[pl.ds(base + row * PAIR, PAIR), :] = table[source, pl.ds(pair * PAIR, PAIR), :]

        def arrivals(which, k, side):
            found = [
                (index, which, source, k, side)
                for step in WAYS[axes(index)[which]]
                for source, target in step
                if target == k and side in both_ways(index, which, source)
            ]
            for key in found:
                copies[key].wait_recv()
            return found

        def region(k, side):
            return OWN[index] + (k if side == 0 else (n - k) % n) * m * tall

        if stage == 3:
            kept = [(0, 0, m, 0)]
            for k, side, count, skip in kept if turn < 0 else [
                (k, side, *((half, side * half) if 2 * k == n else (m, 0)))
                for k, _ in WAYS[first, way][turn]
                for side in range(2)
            ]:
                dest = lax.rem(at[first] + (k if side == 0 else n - k), n)

                def body(item, carry):
                    gather(dest, item + skip, pl.multiple_of(region(k, side) + (item + skip) * tall, 16))
                    return carry

                lax.fori_loop(0, count, body, 0)
        elif stage == 0:
            for k, j, side in ((k, j, side) for k, j in WAYS[first, way][turn] for side in range(2)):
                count, skip = (half, side * half) if 2 * k == n else (m, 0)
                place = PLACE[(index, 0, k, j, side)]
                found = arrivals(0, k, side)
                short = [PLACE[key][1] for key in found if 2 * key[2] == n]
                full = [PLACE[key][1] for key in found if 2 * key[2] != n]

                def put(item, partly):
                    value = own[block(region(k, side), item + skip), :]
                    for offset in full:
                        value = value + got[block(offset, item), :].astype(F32)
                    for offset in short if partly is not None else ():
                        value = value + got[block(offset, partly), :].astype(F32)
                    sent[block(place[1], item), :] = value.astype(BF16)

                if short:
                    def fill(item, carry):
                        put(side * half + item, item)
                        put((1 - side) * half + item, None)
                        return carry

                    lax.fori_loop(0, half, fill, 0)
                else:
                    def fill(item, carry):
                        put(item, None)
                        return carry

                    lax.fori_loop(0, count, fill, 0)
                send((index, 0, k, j, side), place, device(first, k - j if side == 0 else j - k))
        elif stage == 1 and turn == 0:
            arrived = [PLACE[key][1] for side in range(2) for key in arrivals(0, 0, side)]

            def value(item):
                here = own[block(region(0, 0), item), :]
                for offset in arrived:
                    here = here + got[block(offset, item), :].astype(F32)
                return here

            targets = dict(WAYS[other, other_way][0])
            for k in (*sorted(targets, reverse=True), *(k for k in range(1, half + 1) if k not in targets)):
                for side in both_ways(index, 1, k):
                    here = value(lax.rem(at[other] + (k if side == 0 else m - k), m))
                    if k in targets:
                        j = targets[k]
                        place = PLACE[(index, 1, k, j, side)]
                        sent[pl.ds(place[1], tall), :] = here.astype(BF16)
                        send((index, 1, k, j, side), place, device(other, k - j if side == 0 else j - k))
                    else:
                        held[pl.ds(((index * half + k - 1) * 2 + side) * TALL, tall), :] = here
            mine[home, :] = value(at[other])
        elif stage == 1:
            for k, j in WAYS[other, other_way][turn]:
                for side in both_ways(index, 1, k):
                    here = held[pl.ds(((index * half + k - 1) * 2 + side) * TALL, tall), :]
                    for key in arrivals(1, k, side):
                        here = here + got[pl.ds(PLACE[key][1], tall), :].astype(F32)
                    place = PLACE[(index, 1, k, j, side)]
                    sent[pl.ds(place[1], tall), :] = here.astype(BF16)
                    send((index, 1, k, j, side), place, device(other, k - j if side == 0 else j - k))
        else:
            here = mine[home, :]
            for side in range(2):
                for key in arrivals(1, 0, side):
                    here = here + got[pl.ds(PLACE[key][1], tall), :].astype(F32)
            pick[home, :] = here.astype(BF16)
            place = (len(PLACE) + 1 + index, pair * ATT * PAIR + start * PAIR, tall)
            tails[pair].append(send((index, "pick"), place, before, pick, pick_got))

    def factor(otm_ref, side):
        picked = wide[pl.ds(side, ATT, stride=PAIR), :].astype(BF16)
        return lax.dot_general(
            otm_ref[...], picked, (((0,), (0,)), ((), ())), preferred_element_type=F32
        ).astype(BF16)

    def spectra(left, right):
        return lax.dot_general(left, right, (((1,), (1,)), ((), ())), preferred_element_type=F32) * (1.0 / 64.0)

    def direct(pair):
        wide[...] = pick[pl.ds(pair * ATT * PAIR, ATT * PAIR), :].astype(F32)
        for side in range(PAIR):
            line = pair * PAIR + side
            here = factor(otm, side)
            lane = lax.broadcasted_iota(jnp.int32, here.shape, 1)
            turned = pltpu.roll(here.astype(F32), 64, 1)
            turned = jnp.where(lane < 64, turned, -turned).astype(BF16)
            csd_ref[0, line, 0] = spectra(here, here).astype(BF16)
            csd_ref[0, line, 1] = spectra(turned, here).astype(BF16)
            crossing[line, 0] = here[:CROSS]
            crossing[line, 1] = turned[:CROSS]

    def joint(pair):
        for copy in tails[pair]:
            copy.wait_recv()
        arrived = pick_got[pl.ds(pair * ATT * PAIR, ATT * PAIR), :].astype(F32)
        wide[...] = jnp.where(me == NY * NZ - 1, 0.0, arrived)
        for side in range(PAIR):
            line = pair * PAIR + side
            following = factor(otm_got, side)
            for part in range(2):
                joint_ref[0, line, part] = spectra(crossing[line, part], following).astype(BF16)

    for index, stage, turn in ORDER:
        if index >= 0:
            event(index, stage, turn)
        elif turn == 0:
            loads[7 + PIECES].wait()
            products(1)
        elif turn == 1:
            direct(0)
        else:
            loads[5 + PIECES].wait()
            loads[6 + PIECES].wait()
            keep = lax.broadcasted_iota(jnp.int32, otm.shape, 1) < count_smem[0]
            otm[...] = jnp.where(keep, otm[...].astype(F32), 0.0).astype(BF16)
            otm_copy = pltpu.make_async_remote_copy(
                src_ref=otm, dst_ref=otm_got, send_sem=send_sems.at[len(PLACE)],
                recv_sem=recv_sems.at[len(PLACE)], device_id={"mode": before}, device_id_type=MESH)
            otm_copy.start()
    direct(LINES // PAIR - 1)
    otm_copy.wait_recv()
    for pair in range(LINES // PAIR):
        joint(pair)
    for copy in (*copies.values(), otm_copy):
        copy.wait_send()


def store(csd_ref, joint_ref, csd_hbm, joint_hbm, sems):
    copies = []
    for line in range(LINES):
        copies.append(pltpu.make_async_copy(csd_ref.at[0, line], csd_hbm.at[0, line], sems.at[2 * line]))
        copies.append(pltpu.make_async_copy(joint_ref.at[0, line], joint_hbm.at[0, line], sems.at[2 * line + 1]))
    for copy in copies:
        copy.start()
    for copy in copies:
        copy.wait()


def per_device(mode_shapes, modal_freq, damping, excitation, modal_load, attach, row_count, otm):
    iface, modes = mode_shapes.shape
    rows_max, width = otm.shape[1], modal_load.shape[3]
    columns = LINES * 2 * width
    vmem = pl.BlockSpec(memory_space=pltpu.VMEM)
    hbm = pl.BlockSpec(memory_space=pltpu.HBM)
    operands = (
        modal_freq,
        damping,
        excitation,
        modal_load.transpose(1, 2, 3, 0).reshape(columns, modes),
        attach,
        row_count,
        otm[0].T,
        mode_shapes,
    )
    spectra = pl.pallas_call(
            kernel,
            out_shape=[
                jax.ShapeDtypeStruct((1, LINES, 2, rows_max, rows_max), BF16),
                jax.ShapeDtypeStruct((1, LINES, 2, CROSS, rows_max), BF16),
            ],
            in_specs=[hbm] * 8,
            out_specs=[vmem] * 2,
            scratch_shapes=[
                pltpu.VMEM((modes,), F32),
                pltpu.VMEM((modes,), F32),
                pltpu.SMEM((LINES,), F32),
                pltpu.VMEM((columns, modes), F32),
                pltpu.SMEM((COMPS, ATT), jnp.int32),
                pltpu.SMEM((1,), jnp.int32),
                pltpu.VMEM((ATT, rows_max), BF16),
                pltpu.VMEM((iface, modes), BF16),
                pltpu.VMEM((modes, columns), BF16),
                pltpu.VMEM((iface * LINES, 128), F32),
                pltpu.VMEM((COMPS * ATT * LINES, 128), F32),
                pltpu.VMEM((len(CHUNKS) * NZ * TALL, 128), F32),
                pltpu.VMEM((ATT * LINES, 128), F32),
                pltpu.VMEM((TOTAL, 128), BF16),
                pltpu.VMEM((TOTAL, 128), BF16),
                pltpu.VMEM((ATT, rows_max), BF16),
                pltpu.VMEM((ATT * LINES, 128), BF16),
                pltpu.VMEM((ATT * LINES, 128), BF16),
                pltpu.VMEM((ATT * PAIR, 128), F32),
                pltpu.VMEM((LINES, 2, CROSS, 128), BF16),
                pltpu.SemaphoreType.DMA((8 + PIECES,)),
                pltpu.SemaphoreType.DMA((SLOTS,)),
                pltpu.SemaphoreType.DMA((SLOTS,)),
            ],
            compiler_params=pltpu.CompilerParams(
                vmem_limit_bytes=42 << 20, collective_id=0, has_side_effects=True
            ),
            name="loads",
        )(*(value if value is row_count else pltpu.with_memory_space_constraint(value, pltpu.HBM) for value in operands))
    return tuple(
        pl.pallas_call(
            store,
            out_shape=[jax.ShapeDtypeStruct(value.shape, BF16) for value in spectra],
            in_specs=[vmem] * 2,
            out_specs=[hbm] * 2,
            scratch_shapes=[pltpu.SemaphoreType.DMA((2 * LINES,))],
            compiler_params=pltpu.CompilerParams(vmem_limit_bytes=1 << 20),
            name="store",
        )(*spectra)
    )


def solution(mesh):
    return jax.shard_map(
        per_device,
        mesh=mesh,
        in_specs=(
            P(None, "mode"),
            P("mode"),
            P("mode"),
            P("freq"),
            P("mode", "freq", None, None),
            P(),
            P("mode"),
            P("mode", None, None),
        ),
        out_specs=(P("mode", "freq", None, None, None), P("mode", "freq", None, None, None)),
        check_vma=False,
    )
```

```python
import jax
import jax.numpy as jnp
from jax import lax
from jax.experimental import pallas as pl
from jax.experimental.pallas import tpu as pltpu
from jax.sharding import PartitionSpec as P

MESH = pl.DeviceIdType.MESH
F32, BF16 = jnp.float32, jnp.bfloat16
NY, NZ = 4, 8
SIZE = {"y": NY, "z": NZ}
OTHER = {"y": "z", "z": "y"}
COMPS, ATT, LINES, CROSS = 32, 96, 4, 128
CUTS = (0, 768, 2304, 4224, 6144)
PIECES = len(CUTS) - 1
WAYS = {
    ("z", 4): (((4, 3),), ((3, 2),), ((2, 1),), ((1, 0),)),
    ("z", 3): (((4, 2), (3, 2)), ((2, 1),), ((1, 0),)),
    ("z", 2): (((4, 2), (3, 2), (1, 0)), ((2, 0),)),
    ("z", 1): (((4, 0), (3, 0), (2, 0), (1, 0)),),
    ("y", 2): (((2, 1),), ((1, 0),)),
    ("y", 1): (((2, 0), (1, 0)),),
}
CHUNKS = (
    ("z", 4, 1, 0, 0, 16), ("y", 2, 3, 0, 16, 16), ("z", 3, 1, 0, 32, 16), ("z", 4, 1, 0, 48, 16),
    ("y", 2, 2, 0, 64, 16), ("y", 2, 1, 0, 80, 16),
)
ORDER = (
    (0, 3, 0), (0, 0, 0), (1, 3, 0), (1, 0, 0), (3, 3, 0), (3, 0, 0), (2, 3, 0), (2, 0, 0), (4, 3, 0),
    (4, 0, 0), (5, 3, 0), (5, 0, 0), (-1, 0, 2), (0, 3, 1), (3, 3, 1), (1, 3, 1), (0, 0, 1), (4, 3, 1),
    (2, 3, 1), (3, 0, 1), (1, 0, 1), (5, 3, 1), (0, 3, 2), (3, 3, 2), (1, 3, -1), (4, 3, -1), (4, 0, 1),
    (2, 0, 1), (2, 3, 2), (5, 3, -1), (5, 0, 1), (0, 0, 2), (0, 3, 3), (3, 3, 3), (3, 3, -1), (2, 3, -1),
    (0, 3, -1), (3, 0, 2), (1, 1, 0), (2, 0, 2), (0, 0, 3), (4, 1, 0), (3, 0, 3), (1, 1, 1), (5, 1, 0),
    (2, 1, 0), (0, 1, 0), (4, 1, 1), (3, 1, 0), (1, 1, 2), (2, 2, 0), (0, 2, 0), (5, 2, 0), (1, 2, 0),
    (4, 2, 0), (3, 2, 0),
)
PAIR = 4
TALL = max(chunk[-1] for chunk in CHUNKS) * PAIR


def axes(index):
    first, way, other_way = CHUNKS[index][:3]
    return ((first, way), (OTHER[first], other_way))


def both_ways(index, stage, k):
    opposite = 2 * k == SIZE[axes(index)[stage][0]]
    return (index % 2,) if stage == 1 and opposite else (0, 1)


def plan():
    place, total = {}, 0
    for index, chunk in enumerate(CHUNKS):
        tall = chunk[-1] * PAIR
        for stage, way in enumerate(axes(index)):
            for k, j in (copy for turn in WAYS[way] for copy in turn):
                size = tall
                if stage == 0:
                    size *= SIZE[OTHER[way[0]]]
                    size //= 2 if 2 * k == SIZE[way[0]] else 1
                for side in both_ways(index, stage, k):
                    place[(index, stage, k, j, side)] = (len(place), total, size)
                    total += size
    return place, total


PLACE, TOTAL = plan()
OWN = [sum(chunk[-1] for chunk in CHUNKS[:index]) * PAIR * COMPS for index in range(len(CHUNKS))]
SLOTS = len(PLACE) + 1 + len(CHUNKS)


def kernel(freq_hbm, damp_hbm, exc_hbm, load_hbm, attach_hbm, count_hbm, otm_hbm, shapes_hbm, csd_ref, joint_ref,
           freq, damp, exc_smem, load, attach, count_smem, otm, shapes, resp, whole, own, held, mine, sent, got,
           otm_got, pick, pick_got, wide, crossing, in_sems, send_sems, recv_sems):
    me = lax.axis_index("mode")
    at = {"y": me // NZ, "z": lax.rem(me, NZ)}

    def device(axis, offset):
        if axis == "z":
            return at["y"] * NZ + lax.rem(at["z"] + offset + NZ, NZ)
        return lax.rem(at["y"] + offset + NY, NY) * NZ + at["z"]

    before = lax.rem(me + NY * NZ - 1, NY * NZ)
    after = lax.rem(me + 1, NY * NZ)
    parts = [pl.ds(low, high - low) for low, high in zip(CUTS, CUTS[1:])]
    halves = [pl.ds(pair * PAIR * 128, PAIR * 128) for pair in range(LINES // PAIR)]
    moves = [(freq_hbm, freq), (damp_hbm, damp), (exc_hbm, exc_smem), (load_hbm.at[halves[0]], load.at[halves[0]])]
    moves += [(shapes_hbm.at[part], shapes.at[part]) for part in parts]
    moves += [(attach_hbm, attach), (otm_hbm, otm), (count_hbm, count_smem)]
    moves += [(load_hbm.at[half], load.at[half]) for half in halves[1:]]
    loads = [pltpu.make_async_copy(src, dst, in_sems.at[k]) for k, (src, dst) in enumerate(moves)]
    for copy in loads:
        copy.start()
    barrier = pltpu.get_barrier_semaphore()
    peers = [device("z", step) for step in range(1, NZ)] + [device("y", step) for step in range(1, NY)]
    for peer in (*peers, before, after):
        pl.semaphore_signal(barrier, inc=1, device_id={"mode": peer}, device_id_type=MESH)
    for copy in loads[:4]:
        copy.wait()
    omega = freq[...].reshape(1, -1)
    ratio = damp[...].reshape(1, -1)
    omega_sq = omega * omega

    def products(pair):
        for line in range(pair * PAIR, pair * PAIR + PAIR):
            exc = exc_smem[line]
            a = omega_sq - exc * exc
            b = 2.0 * ratio * omega * exc
            denom = a * a + b * b
            frf_re = omega_sq * a / denom
            frf_im = -omega_sq * b / denom
            load_re = load[pl.ds(line * 128, 64), :]
            load_im = load[pl.ds(line * 128 + 64, 64), :]
            parted = [frf_re * load_re - frf_im * load_im, frf_re * load_im + frf_im * load_re]
            resp[:, pl.ds(line * 128, 128)] = jnp.concatenate(parted, axis=0).astype(BF16).T
        for piece in range(PIECES):
            if pair == 0:
                loads[4 + piece].wait()
            block = lax.dot_general(
                shapes[parts[piece], :], resp[:, halves[pair]], (((1,), (0,)), ((), ())), preferred_element_type=F32
            )
            for side in range(PAIR):
                place = pl.ds(CUTS[piece] * LINES + pair * PAIR + side, CUTS[piece + 1] - CUTS[piece], stride=LINES)
                whole[place, :] = block[:, side * 128 : side * 128 + 128]

    products(0)
    loads[4 + PIECES].wait()
    pl.semaphore_wait(barrier, len(peers) + 2)
    copies, tails = {}, [[] for _ in range(LINES // PAIR)]
    table = whole.reshape(whole.shape[0] // LINES, LINES, 128)

    def send(key, place, target, source=sent, dest=got):
        number, offset, size = place
        part = pl.ds(offset, size)
        copy = pltpu.make_async_remote_copy(
            src_ref=source.at[part], dst_ref=dest.at[part], send_sem=send_sems.at[number],
            recv_sem=recv_sems.at[number], device_id={"mode": target}, device_id_type=MESH)
        copy.start()
        copies[key] = copy
        return copy

    def event(index, stage, turn):
        pair, start, rows = CHUNKS[index][3:]
        (first, way), (other, other_way) = axes(index)
        n, m, tall = SIZE[first], SIZE[other], rows * PAIR
        half = m // 2
        home = pl.ds(pair * ATT * PAIR + start * PAIR, tall)

        def block(offset, item):
            return pl.ds(pl.multiple_of(offset + item * tall, 16), tall)

        def gather(dest, item, base):
            unit = item * NZ + dest if first == "z" else dest * NZ + item
            for row in range(rows):
                source = attach[unit, start + row]
                own[pl.ds(base + row * PAIR, PAIR), :] = table[source, pl.ds(pair * PAIR, PAIR), :]

        def arrivals(which, k, side):
            found = [
                (index, which, source, k, side)
                for step in WAYS[axes(index)[which]]
                for source, target in step
                if target == k and side in both_ways(index, which, source)
            ]
            for key in found:
                copies[key].wait_recv()
            return found

        def region(k, side):
            return OWN[index] + (k if side == 0 else (n - k) % n) * m * tall

        if stage == 3:
            kept = [(0, 0, m, 0)]
            for k, side, count, skip in kept if turn < 0 else [
                (k, side, *((half, side * half) if 2 * k == n else (m, 0)))
                for k, _ in WAYS[first, way][turn]
                for side in range(2)
            ]:
                dest = lax.rem(at[first] + (k if side == 0 else n - k), n)

                def body(item, carry):
                    gather(dest, item + skip, pl.multiple_of(region(k, side) + (item + skip) * tall, 16))
                    return carry

                lax.fori_loop(0, count, body, 0)
        elif stage == 0:
            for k, j, side in ((k, j, side) for k, j in WAYS[first, way][turn] for side in range(2)):
                count, skip = (half, side * half) if 2 * k == n else (m, 0)
                place = PLACE[(index, 0, k, j, side)]
                found = arrivals(0, k, side)
                short = [PLACE[key][1] for key in found if 2 * key[2] == n]
                full = [PLACE[key][1] for key in found if 2 * key[2] != n]

                def put(item, partly):
                    value = own[block(region(k, side), item + skip), :]
                    for offset in full:
                        value = value + got[block(offset, item), :].astype(F32)
                    for offset in short if partly is not None else ():
                        value = value + got[block(offset, partly), :].astype(F32)
                    sent[block(place[1], item), :] = value.astype(BF16)

                if short:
                    def fill(item, carry):
                        put(side * half + item, item)
                        put((1 - side) * half + item, None)
                        return carry

                    lax.fori_loop(0, half, fill, 0)
                else:
                    def fill(item, carry):
                        put(item, None)
                        return carry

                    lax.fori_loop(0, count, fill, 0)
                send((index, 0, k, j, side), place, device(first, k - j if side == 0 else j - k))
        elif stage == 1 and turn == 0:
            arrived = [PLACE[key][1] for side in range(2) for key in arrivals(0, 0, side)]

            def value(item):
                here = own[block(region(0, 0), item), :]
                for offset in arrived:
                    here = here + got[block(offset, item), :].astype(F32)
                return here

            targets = dict(WAYS[other, other_way][0])
            for k in (*sorted(targets, reverse=True), *(k for k in range(1, half + 1) if k not in targets)):
                for side in both_ways(index, 1, k):
                    here = value(lax.rem(at[other] + (k if side == 0 else m - k), m))
                    if k in targets:
                        j = targets[k]
                        place = PLACE[(index, 1, k, j, side)]
                        sent[pl.ds(place[1], tall), :] = here.astype(BF16)
                        send((index, 1, k, j, side), place, device(other, k - j if side == 0 else j - k))
                    else:
                        held[pl.ds(((index * half + k - 1) * 2 + side) * TALL, tall), :] = here
            mine[home, :] = value(at[other])
        elif stage == 1:
            for k, j in WAYS[other, other_way][turn]:
                for side in both_ways(index, 1, k):
                    here = held[pl.ds(((index * half + k - 1) * 2 + side) * TALL, tall), :]
                    for key in arrivals(1, k, side):
                        here = here + got[pl.ds(PLACE[key][1], tall), :].astype(F32)
                    place = PLACE[(index, 1, k, j, side)]
                    sent[pl.ds(place[1], tall), :] = here.astype(BF16)
                    send((index, 1, k, j, side), place, device(other, k - j if side == 0 else j - k))
        else:
            here = mine[home, :]
            for side in range(2):
                for key in arrivals(1, 0, side):
                    here = here + got[pl.ds(PLACE[key][1], tall), :].astype(F32)
            pick[home, :] = here.astype(BF16)
            place = (len(PLACE) + 1 + index, pair * ATT * PAIR + start * PAIR, tall)
            tails[pair].append(send((index, "pick"), place, before, pick, pick_got))

    def factor(otm_ref, side):
        picked = wide[pl.ds(side, ATT, stride=PAIR), :].astype(BF16)
        return lax.dot_general(
            otm_ref[...], picked, (((0,), (0,)), ((), ())), preferred_element_type=F32
        ).astype(BF16)

    def spectra(left, right):
        return lax.dot_general(left, right, (((1,), (1,)), ((), ())), preferred_element_type=F32) * (1.0 / 64.0)

    def direct(pair):
        wide[...] = pick[pl.ds(pair * ATT * PAIR, ATT * PAIR), :].astype(F32)
        for side in range(PAIR):
            line = pair * PAIR + side
            here = factor(otm, side)
            lane = lax.broadcasted_iota(jnp.int32, here.shape, 1)
            turned = pltpu.roll(here.astype(F32), 64, 1)
            turned = jnp.where(lane < 64, turned, -turned).astype(BF16)
            csd_ref[0, line, 0] = spectra(here, here).astype(BF16)
            csd_ref[0, line, 1] = spectra(turned, here).astype(BF16)
            crossing[line, 0] = here[:CROSS]
            crossing[line, 1] = turned[:CROSS]

    def joint(pair):
        for copy in tails[pair]:
            copy.wait_recv()
        arrived = pick_got[pl.ds(pair * ATT * PAIR, ATT * PAIR), :].astype(F32)
        wide[...] = jnp.where(me == NY * NZ - 1, 0.0, arrived)
        for side in range(PAIR):
            line = pair * PAIR + side
            following = factor(otm_got, side)
            for part in range(2):
                joint_ref[0, line, part] = spectra(crossing[line, part], following).astype(BF16)

    for index, stage, turn in ORDER:
        if index >= 0:
            event(index, stage, turn)
        elif turn == 0:
            loads[7 + PIECES].wait()
            products(1)
        elif turn == 1:
            direct(0)
        else:
            loads[5 + PIECES].wait()
            loads[6 + PIECES].wait()
            keep = lax.broadcasted_iota(jnp.int32, otm.shape, 1) < count_smem[0]
            otm[...] = jnp.where(keep, otm[...].astype(F32), 0.0).astype(BF16)
            otm_copy = pltpu.make_async_remote_copy(
                src_ref=otm, dst_ref=otm_got, send_sem=send_sems.at[len(PLACE)],
                recv_sem=recv_sems.at[len(PLACE)], device_id={"mode": before}, device_id_type=MESH)
            otm_copy.start()
    direct(LINES // PAIR - 1)
    otm_copy.wait_recv()
    for pair in range(LINES // PAIR):
        joint(pair)
    for copy in (*copies.values(), otm_copy):
        copy.wait_send()


def store(csd_ref, joint_ref, csd_hbm, joint_hbm, sems):
    copies = []
    for line in range(LINES):
        copies.append(pltpu.make_async_copy(csd_ref.at[0, line], csd_hbm.at[0, line], sems.at[2 * line]))
        copies.append(pltpu.make_async_copy(joint_ref.at[0, line], joint_hbm.at[0, line], sems.at[2 * line + 1]))
    for copy in copies:
        copy.start()
    for copy in copies:
        copy.wait()


def per_device(mode_shapes, modal_freq, damping, excitation, modal_load, attach, row_count, otm):
    iface, modes = mode_shapes.shape
    rows_max, width = otm.shape[1], modal_load.shape[3]
    columns = LINES * 2 * width
    vmem = pl.BlockSpec(memory_space=pltpu.VMEM)
    hbm = pl.BlockSpec(memory_space=pltpu.HBM)
    operands = (
        modal_freq,
        damping,
        excitation,
        modal_load.transpose(1, 2, 3, 0).reshape(columns, modes),
        attach,
        row_count,
        otm[0].T,
        mode_shapes,
    )
    spectra = pl.pallas_call(
            kernel,
            out_shape=[
                jax.ShapeDtypeStruct((1, LINES, 2, rows_max, rows_max), BF16),
                jax.ShapeDtypeStruct((1, LINES, 2, CROSS, rows_max), BF16),
            ],
            in_specs=[hbm] * 8,
            out_specs=[vmem] * 2,
            scratch_shapes=[
                pltpu.VMEM((modes,), F32),
                pltpu.VMEM((modes,), F32),
                pltpu.SMEM((LINES,), F32),
                pltpu.VMEM((columns, modes), F32),
                pltpu.SMEM((COMPS, ATT), jnp.int32),
                pltpu.SMEM((1,), jnp.int32),
                pltpu.VMEM((ATT, rows_max), BF16),
                pltpu.VMEM((iface, modes), BF16),
                pltpu.VMEM((modes, columns), BF16),
                pltpu.VMEM((iface * LINES, 128), F32),
                pltpu.VMEM((COMPS * ATT * LINES, 128), F32),
                pltpu.VMEM((len(CHUNKS) * NZ * TALL, 128), F32),
                pltpu.VMEM((ATT * LINES, 128), F32),
                pltpu.VMEM((TOTAL, 128), BF16),
                pltpu.VMEM((TOTAL, 128), BF16),
                pltpu.VMEM((ATT, rows_max), BF16),
                pltpu.VMEM((ATT * LINES, 128), BF16),
                pltpu.VMEM((ATT * LINES, 128), BF16),
                pltpu.VMEM((ATT * PAIR, 128), F32),
                pltpu.VMEM((LINES, 2, CROSS, 128), BF16),
                pltpu.SemaphoreType.DMA((8 + PIECES,)),
                pltpu.SemaphoreType.DMA((SLOTS,)),
                pltpu.SemaphoreType.DMA((SLOTS,)),
            ],
            compiler_params=pltpu.CompilerParams(
                vmem_limit_bytes=42 << 20, collective_id=0, has_side_effects=True
            ),
            name="loads",
        )(*(value if value is row_count else pltpu.with_memory_space_constraint(value, pltpu.HBM) for value in operands))
    return tuple(
        pl.pallas_call(
            store,
            out_shape=[jax.ShapeDtypeStruct(value.shape, BF16) for value in spectra],
            in_specs=[vmem] * 2,
            out_specs=[hbm] * 2,
            scratch_shapes=[pltpu.SemaphoreType.DMA((2 * LINES,))],
            compiler_params=pltpu.CompilerParams(vmem_limit_bytes=1 << 20),
            name="store",
        )(*spectra)
    )


def solution(mesh):
    return jax.shard_map(
        per_device,
        mesh=mesh,
        in_specs=(
            P(None, "mode"),
            P("mode"),
            P("mode"),
            P("freq"),
            P("mode", "freq", None, None),
            P(),
            P("mode"),
            P("mode", None, None),
        ),
        out_specs=(P("mode", "freq", None, None, None), P("mode", "freq", None, None, None)),
        check_vma=False,
    )
```
